32 devices in a mesh: head: 4 (over y, core), st: 8 (over z, x).
Axes of the slice: x: 2, y: 2, z: 4, core: 2. Of those that a mesh axis runs over, the one named last changes fastest.
Arguments:
- queries: bfloat16 [8, 1024, 40, 128], P('st', 'head'), may hold values from -68 to 68
- key_vectors: bfloat16 [8, 1024, 40, 128], P('st', 'head'), may hold values from -14 to 14
- value_vectors: bfloat16 [8, 1024, 40, 128], P('st', 'head'), may hold values from -4.5 to 4.5
- block_lists: int32 [64, 40, 8], P('st', 'head'), may hold values from -1 to 7, as said below
Outputs:
- attended: bfloat16 [8, 1024, 40, 128], P('st', 'head')
The draws below stay inside these ranges and needn't reach their ends.
Inputs may be any that keep to these rules, and one draw needn't show every extreme that they name: `block_lists`: for each query tile and head: the selected key blocks of its own tube in ascending order, each once, then -1 in the remaining entries; the tile's own block (block t for tile t) is always selected; at most 8 blocks, and in every draw some tile selects all 8 blocks in every head.
All inputs are finite; a program needn't handle non-finite values.
Results may differ from the reference program's by a relative error of at most 0.0043.
Values may be sent and summed in bfloat16 or wider, within the bound.
No kernel may reach another device: no remote copies, remote signals or barrier semaphores. Data moves between devices by JAX's collectives and lax.ppermute only.
A program may use at most 128 MiB of HBM per device.

```python
import jax
import jax.numpy as jnp
from jax import lax

HEADS = 40
HDIM = 128
S = 1024
BLK = 128
FRAMES = 8
SUB = 128
NB = 8
TILES = 64
N_ST = 8


def key_field(key):
    raw_keys = jnp.clip(jax.random.normal(jax.random.fold_in(key, 101), (FRAMES, S, HEADS, HDIM), jnp.float32), -4.5, 4.5)
    shaped = raw_keys
    return shaped


def draw_key_vectors(key, part):
    shaped = key_field(key)
    return shaped.astype(jnp.bfloat16)


def draw_queries(key, part):
    query_raw = jnp.clip(jax.random.normal(jax.random.fold_in(key, 201), (FRAMES, S, HEADS, HDIM), jnp.float32), -4.5, 4.5)
    result = query_raw
    return result.astype(jnp.bfloat16)


def draw_block_lists(key, part):
    tube_total = TILES // NB
    heavy_tube = jax.random.randint(jax.random.fold_in(key, 301), (tube_total,), 0, 4) == 0
    light_level = jax.random.randint(jax.random.fold_in(key, 302), (tube_total,), 1, max(NB // 4, 1) + 1)
    tube_level = jnp.where(heavy_tube, NB, light_level)
    tile_level = jnp.repeat(tube_level, NB)
    lowest = (tile_level + 1) // 2
    counts = jax.random.randint(jax.random.fold_in(key, 303), (TILES, HEADS), lowest[:, None], tile_level[:, None] + 1)
    forced = jax.random.randint(jax.random.fold_in(key, 304), (), 0, TILES)
    tile_pos = jnp.arange(TILES)
    counts = jnp.where((tile_pos == forced)[:, None], NB, counts)
    block_pos = jnp.arange(NB)
    ranks_raw = jax.random.randint(jax.random.fold_in(key, 305), (TILES, HEADS, NB), 0, 1 << 20) * NB + block_pos
    own_block = (block_pos[None, :] == (tile_pos % NB)[:, None])[:, None, :]
    ranks_raw = jnp.where(own_block, -1, ranks_raw)
    sorted_idx = jnp.argsort(ranks_raw, axis=2)
    ranking = jnp.argsort(sorted_idx, axis=2)
    chosen = ranking < counts[:, :, None]
    sorting = jnp.sort(jnp.where(chosen, block_pos, NB + block_pos), axis=2)
    return jnp.where(sorting < NB, sorting, -1).astype(jnp.int32)


def level_of(key, dims, cuts, least, largest):
    level, own = 1.0, jax.random.fold_in(key, 6)
    for position, shards_of in cuts:
        draws = jnp.exp(jax.random.uniform(jax.random.fold_in(own, position), (shards_of,), jnp.float32, least / len(cuts), largest / len(cuts)))
        level = level * jnp.repeat(draws, dims[position] // shards_of).reshape([-1 if axis == position else 1 for axis in range(len(dims))])
    return level


def noise(own_key, dims, scale, reach, pieces=(), held_as=jnp.bfloat16):
    array = jax.random.normal(own_key, dims, jnp.float32) * scale
    if len(pieces) > 0:
        array = level_of(own_key, dims, pieces, -0.22, 0.18) * array
    return jnp.clip(array, min=-reach, max=reach).astype(held_as)


def setup_inputs(seed: int = 0) -> dict:
    keys = jax.random.split(jax.random.key(seed), 5)
    return {
        "queries": draw_queries(jax.random.fold_in(keys[4], 71), 0),
        "key_vectors": draw_key_vectors(jax.random.fold_in(keys[4], 71), 0),
        "value_vectors": noise(keys[2], (FRAMES, S, HEADS, HDIM), 1.0, 4.5, ((0, 8), (1, 4))),
        "block_lists": draw_block_lists(jax.random.fold_in(keys[4], 71), 0),
    }


def tube_attention(query_rows, key_rows, value_rows, lists_here):
    row_count, head_count, head_width = query_rows.shape
    blocks = row_count // BLK
    query_wide = query_rows.astype(jnp.float32).reshape(blocks, BLK, head_count, head_width)
    key_wide = key_rows.astype(jnp.float32).reshape(blocks, BLK, head_count, head_width)
    value_wide = value_rows.astype(jnp.float32).reshape(blocks, BLK, head_count, head_width)
    block_pos = jnp.arange(blocks, dtype=jnp.int32)
    picked = jnp.any(lists_here[:, :, :, None] == block_pos[None, None, None, :], axis=2)
    scores = jnp.einsum("tqhd,bkhd->htqbk", query_wide, key_wide) * (head_width ** -0.5)
    allowed = jnp.transpose(picked, (1, 0, 2))[:, :, None, :, None]
    scores = jnp.where(allowed, scores, -jnp.inf)
    row_max = jnp.max(scores, axis=(3, 4), keepdims=True)
    weights = jnp.exp(scores - row_max)
    row_total = jnp.sum(weights, axis=(3, 4))
    rounded = lax.optimization_barrier(weights.astype(jnp.bfloat16)).astype(jnp.float32)
    summed = jnp.einsum("htqbk,bkhd->tqhd", rounded, value_wide)
    result = summed / jnp.transpose(row_total, (1, 2, 0))[..., None]
    return result.reshape(row_count, head_count, head_width).astype(jnp.bfloat16)


def reference(queries, key_vectors, value_vectors, block_lists):
    def one_tube(tube):
        def take_tube(source):
            piece = lax.dynamic_slice_in_dim(source, tube * SUB, SUB, 1)
            return piece.reshape(FRAMES * SUB, HEADS, HDIM)

        lists_here = lax.dynamic_slice_in_dim(block_lists, tube * NB, NB, 0)
        result = tube_attention(take_tube(queries), take_tube(key_vectors), take_tube(value_vectors), lists_here)
        return result.reshape(FRAMES, SUB, HEADS, HDIM)

    tubes = lax.map(one_tube, jnp.arange(N_ST, dtype=jnp.int32))
    return jnp.transpose(tubes, (1, 0, 2, 3, 4)).reshape(FRAMES, S, HEADS, HDIM)
```

```python
import functools

import jax
import jax.numpy as jnp
from jax import lax
from jax.experimental import pallas as pl
from jax.experimental.pallas import tpu as pltpu
from jax.sharding import PartitionSpec as P

BLK = 128


def pack_kernel(q_ref, k_ref, v_ref, out_ref):
    owners, _, held, rows, width = out_ref.shape
    for slot, ref in enumerate((q_ref, k_ref, v_ref)):
        turned = pltpu.einshape("phd->hpd", ref[...])
        out_ref[:, slot] = turned.reshape(owners, held, rows, width)


def pack(queries, key_vectors, value_vectors, first, tubes, rows, devs):
    heads, width = queries.shape[1:]
    held = tubes * heads // devs
    owners = heads // held
    step = min(rows, 32)
    steps = rows // step
    source = pl.BlockSpec((step, heads, width), lambda t, i: ((first + t) * steps + i, 0, 0))
    return pl.pallas_call(
        pack_kernel,
        out_shape=jax.ShapeDtypeStruct((devs, 3, held, rows, width), queries.dtype),
        grid=(tubes, steps),
        in_specs=[source, source, source],
        out_specs=pl.BlockSpec((owners, 3, held, step, width), lambda t, i: (t, 0, 0, i, 0)),
        cost_estimate=pl.CostEstimate(
            flops=0, transcendentals=0, bytes_accessed=12 * devs * held * rows * width
        ),
        name="pack",
    )(queries, key_vectors, value_vectors)


def unpack_kernel(src_ref, *refs):
    out_ref = refs[-1]
    owners, held, rows, width = src_ref.shape
    out_ref[...] = pltpu.einshape("hpd->phd", src_ref[...].reshape(owners * held, rows, width))


def unpack(arrived, out, first, tubes, all_rows):
    devs, held, rows, width = arrived.shape
    owners = devs // tubes
    heads = owners * held
    step = min(rows, 32)
    steps = rows // step
    operands, in_specs, aliases = [arrived], [], {}
    in_specs.append(pl.BlockSpec((owners, held, step, width), lambda t, i: (t, 0, i, 0)))
    if out is not None:
        operands.append(out)
        in_specs.append(pl.BlockSpec(memory_space=pl.ANY))
        aliases = {1: 0}
    return pl.pallas_call(
        unpack_kernel,
        out_shape=jax.ShapeDtypeStruct((all_rows, heads, width), arrived.dtype),
        grid=(tubes, steps),
        in_specs=in_specs,
        out_specs=pl.BlockSpec(
            (step, heads, width), lambda t, i: ((first + t) * steps + i, 0, 0)
        ),
        input_output_aliases=aliases,
        cost_estimate=pl.CostEstimate(
            flops=0, transcendentals=0, bytes_accessed=4 * devs * held * rows * width
        ),
        name="unpack",
    )(*operands)


def attend_kernel(tiles, per_group, base_ref, lists_ref, q_ref, k_ref, v_ref, o_ref):
    frames, rows, width = q_ref.shape
    tokens = frames * rows
    span = BLK // rows
    group = 2
    entries = tokens // BLK
    head = base_ref[1] + pl.program_id(0)
    stride = per_group * entries
    start = base_ref[0] + (head // per_group) * (tiles * stride) + (head % per_group) * entries
    keys = k_ref[...].reshape(tokens, width)
    values = v_ref[...].reshape(tokens, width)
    block_of = lax.broadcasted_iota(jnp.int32, (1, tokens), 1) // BLK
    scale = width ** (-0.5)
    for pair in range(tiles // group):
        query = q_ref[pair * group * span : (pair + 1) * group * span]
        query = query.reshape(group * BLK, width)
        scores = lax.dot_general(
            query, keys, (((1,), (1,)), ((), ())), preferred_element_type=jnp.float32
        )
        parts = []
        for member in range(group):
            tile = pair * group + member
            bits = jnp.int32(0)
            for e in range(entries):
                block = lists_ref[start + tile * stride + e]
                bits = bits | jnp.where(block >= 0, 1 << jnp.maximum(block, 0), 0)
            chosen = ((bits >> block_of) & 1) == 1
            bias = jnp.where(chosen, 0.0, -jnp.inf)
            part = scores[member * BLK : (member + 1) * BLK] * scale + bias
            weights = jnp.exp(part - jnp.max(part, axis=1, keepdims=True))
            total = jnp.sum(weights, axis=1, keepdims=True)
            parts.append((weights.astype(jnp.bfloat16), total))
        rounded = jnp.concatenate([part for part, _ in parts], axis=0)
        totals = jnp.concatenate([total for _, total in parts], axis=0)
        summed = jnp.dot(rounded, values, preferred_element_type=jnp.float32)
        result = (summed / totals).astype(o_ref.dtype)
        o_ref[pair * group * span : (pair + 1) * group * span] = result.reshape(
            group * span, rows, width
        )


def attend(arrived, base, lists, tiles, per_group):
    devs, _, held, rows, width = arrived.shape
    tokens = devs * rows

    def part(slot):
        return pl.BlockSpec((devs, None, None, rows, width), lambda u, *_: (0, slot, u, 0, 0))

    return pl.pallas_call(
        functools.partial(attend_kernel, tiles, per_group),
        out_shape=jax.ShapeDtypeStruct((devs, held, rows, width), arrived.dtype),
        grid_spec=pltpu.PrefetchScalarGridSpec(
            num_scalar_prefetch=2,
            grid=(held,),
            in_specs=[part(0), part(1), part(2)],
            out_specs=pl.BlockSpec((devs, None, rows, width), lambda u, *_: (0, u, 0, 0)),
        ),
        cost_estimate=pl.CostEstimate(
            flops=4 * held * tokens * tokens * width,
            transcendentals=held * tokens * tokens,
            bytes_accessed=8 * held * tokens * width,
        ),
        name="attend",
    )(base, lists, arrived, arrived, arrived)


def exchange(blocks):
    return lax.all_to_all(blocks, "st", split_axis=0, concat_axis=0, tiled=True)


def body(queries, key_vectors, value_vectors, block_lists):
    head_devs = lax.axis_size("head")
    st_devs = lax.axis_size("st")
    local_frames, local_space, heads, width = queries.shape
    plane_tubes = st_devs // head_devs
    rows = local_frames * local_space // plane_tubes
    tiles, per_group, entries = block_lists.shape
    all_rows = local_frames * local_space
    chunk_tubes = 1 if heads % st_devs == 0 else plane_tubes
    held = chunk_tubes * heads // st_devs
    owners = heads // held

    def flat(source):
        shaped = source.reshape(local_frames, plane_tubes, -1, heads, width)
        return jnp.swapaxes(shaped, 0, 1).reshape(all_rows, heads, width)

    q_rows, k_rows, v_rows = flat(queries), flat(key_vectors), flat(value_vectors)
    head_at, st_at = lax.axis_index("head"), lax.axis_index("st")
    lists_all = lax.all_gather(block_lists.reshape(-1), ("st", "head"), axis=0, tiled=True)
    tube_size = tiles * heads * entries
    lists = lax.dynamic_slice(
        lists_all, (head_at * plane_tubes * tube_size,), (plane_tubes * tube_size,)
    )
    out = None
    for first in range(0, plane_tubes, chunk_tubes):
        arrived = exchange(pack(q_rows, k_rows, v_rows, first, chunk_tubes, rows, st_devs))
        base = jnp.stack([(first + st_at // owners) * tube_size, (st_at % owners) * held])
        result = attend(arrived, base, lists, tiles, per_group)
        out = unpack(exchange(result), out, first, chunk_tubes, all_rows)
    shaped = out.reshape(plane_tubes, local_frames, -1, heads, width)
    return jnp.swapaxes(shaped, 0, 1).reshape(queries.shape)


def solution(mesh):
    spec = P("st", "head", None, None)
    return jax.shard_map(
        body,
        mesh=mesh,
        in_specs=(spec, spec, spec, P("st", "head", None)),
        out_specs=spec,
        check_vma=False,
    )
```

```python
import functools

import jax
import jax.numpy as jnp
from jax import lax
from jax.experimental import pallas as pl
from jax.experimental.pallas import tpu as pltpu
from jax.sharding import PartitionSpec as P

BLK = 128


def pack_kernel(devs, tubes, me_ref, q_ref, k_ref, v_ref, *refs):
    outs, turned_ref = refs[:-1], refs[-1]
    held = outs[0].shape[1]
    owners = devs // tubes
    t = pl.program_id(1)
    for part, ref in enumerate((q_ref, k_ref, v_ref)):
        turned_ref[...] = pltpu.einshape("phd->hpd", ref[...])
        for r in range(devs):
            owner = me_ref[0] ^ r

            def write(r=r, owner=owner):
                outs[r][part] = turned_ref[pl.ds((owner % owners) * held, held)]

            if tubes == 1:
                write()
            else:
                pl.when(owner // owners == t)(write)


def pack(me, queries, key_vectors, value_vectors, first, tubes, rows, devs):
    heads, width = queries.shape[1:]
    held = tubes * heads // devs
    step = min(rows, 32)
    steps = rows // step
    source = pl.BlockSpec(
        (step, heads, width), lambda i, t, *_: ((first + t) * steps + i, 0, 0)
    )
    slot = pl.BlockSpec((3, held, step, width), lambda i, t, *_: (0, 0, i, 0))
    return pl.pallas_call(
        functools.partial(pack_kernel, devs, tubes),
        out_shape=[jax.ShapeDtypeStruct((3, held, rows, width), queries.dtype)] * devs,
        grid_spec=pltpu.PrefetchScalarGridSpec(
            num_scalar_prefetch=1,
            grid=(steps, tubes),
            in_specs=[source, source, source],
            out_specs=[slot] * devs,
            scratch_shapes=[pltpu.VMEM((heads, step, width), queries.dtype)],
        ),
        cost_estimate=pl.CostEstimate(
            flops=0, transcendentals=0, bytes_accessed=12 * devs * held * rows * width
        ),
        name="pack",
    )(me, queries, key_vectors, value_vectors)


def unpack_kernel(devs, tubes, me_ref, *refs):
    slots, (out_ref, turned_ref) = refs[:devs], refs[-2:]
    held = slots[0].shape[0]
    owners = devs // tubes
    t = pl.program_id(1)
    for r in range(devs):
        owner = me_ref[0] ^ r

        def read(r=r, owner=owner):
            turned_ref[pl.ds((owner % owners) * held, held)] = slots[r][...]

        if tubes == 1:
            read()
        else:
            pl.when(owner // owners == t)(read)
    out_ref[...] = pltpu.einshape("hpd->phd", turned_ref[...])


def unpack(me, arrived, out, first, tubes, all_rows):
    devs = len(arrived)
    held, rows, width = arrived[0].shape
    heads = devs * held // tubes
    step = min(rows, 32)
    steps = rows // step
    operands = [me, *arrived]
    in_specs = [pl.BlockSpec((held, step, width), lambda i, t, *_: (0, i, 0))] * devs
    aliases = {}
    if out is not None:
        operands.append(out)
        in_specs.append(pl.BlockSpec(memory_space=pl.ANY))
        aliases = {len(operands) - 1: 0}
    return pl.pallas_call(
        functools.partial(unpack_kernel, devs, tubes),
        out_shape=jax.ShapeDtypeStruct((all_rows, heads, width), arrived[0].dtype),
        grid_spec=pltpu.PrefetchScalarGridSpec(
            num_scalar_prefetch=1,
            grid=(steps, tubes),
            in_specs=in_specs,
            out_specs=pl.BlockSpec(
                (step, heads, width), lambda i, t, *_: ((first + t) * steps + i, 0, 0)
            ),
            scratch_shapes=[pltpu.VMEM((heads, step, width), arrived[0].dtype)],
        ),
        input_output_aliases=aliases,
        cost_estimate=pl.CostEstimate(
            flops=0, transcendentals=0, bytes_accessed=4 * devs * held * rows * width
        ),
        name="unpack",
    )(*operands)


def attend_kernel(devs, tiles, per_group, base_ref, lists_ref, *refs):
    slots, outs = refs[:devs], refs[devs:]
    _, rows, width = slots[0].shape
    span = BLK // rows
    group = 2
    entries = devs // span
    tokens = devs * rows
    turn = base_ref[2] // span
    head = base_ref[1] + pl.program_id(0)
    stride = per_group * entries
    start = base_ref[0] + (head // per_group) * (tiles * stride) + (head % per_group) * entries
    keys = jnp.concatenate([ref[1] for ref in slots], axis=0)
    values = jnp.concatenate([ref[2] for ref in slots], axis=0)
    block_of = (lax.broadcasted_iota(jnp.int32, (1, tokens), 1) // BLK) ^ turn
    scale = width ** (-0.5)
    for pair in range(tiles // group):
        here = range(pair * group * span, (pair + 1) * group * span)
        query = jnp.concatenate([slots[r][0] for r in here], axis=0)
        scores = lax.dot_general(
            query, keys, (((1,), (1,)), ((), ())), preferred_element_type=jnp.float32
        )
        parts = []
        for member in range(group):
            tile = (pair * group + member) ^ turn
            bits = jnp.int32(0)
            for e in range(entries):
                block = lists_ref[start + tile * stride + e]
                bits = bits | jnp.where(block >= 0, 1 << jnp.maximum(block, 0), 0)
            chosen = ((bits >> block_of) & 1) == 1
            bias = jnp.where(chosen, 0.0, -jnp.inf)
            part = scores[member * BLK : (member + 1) * BLK] * scale + bias
            weights = jnp.exp(part - jnp.max(part, axis=1, keepdims=True))
            total = jnp.sum(weights, axis=1, keepdims=True)
            parts.append((weights.astype(jnp.bfloat16), total))
        rounded = jnp.concatenate([part for part, _ in parts], axis=0)
        totals = jnp.concatenate([total for _, total in parts], axis=0)
        summed = jnp.dot(rounded, values, preferred_element_type=jnp.float32)
        result = (summed / totals).astype(outs[0].dtype)
        for place, r in enumerate(here):
            outs[r][...] = result[place * rows : (place + 1) * rows]


def attend(arrived, base, lists, tiles, per_group):
    devs = len(arrived)
    _, held, rows, width = arrived[0].shape
    tokens = devs * rows
    return pl.pallas_call(
        functools.partial(attend_kernel, devs, tiles, per_group),
        out_shape=[jax.ShapeDtypeStruct((held, rows, width), arrived[0].dtype)] * devs,
        grid_spec=pltpu.PrefetchScalarGridSpec(
            num_scalar_prefetch=2,
            grid=(held,),
            in_specs=[pl.BlockSpec((3, None, rows, width), lambda u, *_: (0, u, 0, 0))] * devs,
            out_specs=[pl.BlockSpec((None, rows, width), lambda u, *_: (u, 0, 0))] * devs,
        ),
        cost_estimate=pl.CostEstimate(
            flops=4 * held * tokens * tokens * width,
            transcendentals=held * tokens * tokens,
            bytes_accessed=8 * held * tokens * width,
        ),
        name="attend",
    )(base, lists, *arrived)


def attend_own_kernel(devs, *refs):
    slots, outs = refs[:devs], refs[devs:]
    scale = slots[0].shape[-1] ** (-0.5)
    for ref, out_ref in zip(slots, outs):
        scores = lax.dot_general(
            ref[0], ref[1], (((1,), (1,)), ((), ())), preferred_element_type=jnp.float32
        )
        scores = scores * scale
        weights = jnp.exp(scores - jnp.max(scores, axis=1, keepdims=True))
        total = jnp.sum(weights, axis=1, keepdims=True)
        summed = jnp.dot(
            weights.astype(jnp.bfloat16), ref[2], preferred_element_type=jnp.float32
        )
        out_ref[...] = (summed / total).astype(out_ref.dtype)


def attend_own(packed):
    devs = len(packed)
    _, held, rows, width = packed[0].shape
    return pl.pallas_call(
        functools.partial(attend_own_kernel, devs),
        out_shape=[jax.ShapeDtypeStruct((held, rows, width), packed[0].dtype)] * devs,
        grid=(held,),
        in_specs=[pl.BlockSpec((3, None, rows, width), lambda u: (0, u, 0, 0))] * devs,
        out_specs=[pl.BlockSpec((None, rows, width), lambda u: (u, 0, 0))] * devs,
        cost_estimate=pl.CostEstimate(
            flops=4 * devs * held * rows * rows * width,
            transcendentals=devs * held * rows * rows,
            bytes_accessed=8 * devs * held * rows * width,
        ),
        name="attend_own",
    )(*packed)


def exchange(slots):
    devs = len(slots)
    far_first = sorted(range(1, devs), reverse=True)
    moved = {
        r: lax.ppermute(slots[r], "st", [(s, s ^ r) for s in range(devs)]) for r in far_first
    }
    return [slots[0]] + [moved[r] for r in range(1, devs)]


def body(queries, key_vectors, value_vectors, block_lists):
    head_devs = lax.axis_size("head")
    st_devs = lax.axis_size("st")
    local_frames, local_space, heads, width = queries.shape
    plane_tubes = st_devs // head_devs
    rows = local_frames * local_space // plane_tubes
    tiles, per_group, entries = block_lists.shape
    all_rows = local_frames * local_space
    chunk_tubes = 1 if heads % st_devs == 0 else plane_tubes
    held = chunk_tubes * heads // st_devs
    owners = st_devs // chunk_tubes
    chunks = plane_tubes // chunk_tubes

    def flat(source):
        shaped = source.reshape(local_frames, plane_tubes, -1, heads, width)
        return jnp.swapaxes(shaped, 0, 1).reshape(all_rows, heads, width)

    tensors = flat(queries), flat(key_vectors), flat(value_vectors)
    head_at, st_at = lax.axis_index("head"), lax.axis_index("st")
    me = jnp.stack([st_at])
    lists_all = lax.all_gather(block_lists.reshape(-1), ("st", "head"), axis=0, tiled=True)
    tube_size = tiles * heads * entries
    lists = lax.dynamic_slice(
        lists_all, (head_at * plane_tubes * tube_size,), (plane_tubes * tube_size,)
    )

    def run(travels, tensors, lists):
        packed = [
            pack(me, *tensors, c * chunk_tubes, chunk_tubes, rows, st_devs)
            for c in range(chunks)
        ]
        arrived = [exchange(p) if t else None for p, t in zip(packed, travels)]
        out = None
        for c in range(chunks):
            if travels[c]:
                base = jnp.stack(
                    [(c + st_at // owners) * tube_size, (st_at % owners) * held, st_at]
                )
                result = exchange(attend(arrived[c], base, lists, tiles, per_group))
            else:
                result = attend_own(packed[c])
            out = unpack(me, result, out, c * chunk_tubes, chunk_tubes, all_rows)
        return out

    if rows % BLK == 0 and tiles == st_devs and chunk_tubes == 1 and plane_tubes <= 2:
        tile_of = (jnp.arange(per_group * tiles * entries) // (per_group * entries))[None]
        shaped = lists.reshape(plane_tubes * head_devs, -1)
        own = jnp.all((shaped == tile_of) | (shaped == -1), axis=1)
        own = jnp.all(own.reshape(plane_tubes, head_devs), axis=1)
        which = jnp.sum(jnp.where(own, 0, 1 << jnp.arange(plane_tubes)))
        branches = [
            functools.partial(run, [bool((code >> c) & 1) for c in range(chunks)])
            for code in range(1 << plane_tubes)
        ]
        out = lax.switch(which, branches, tensors, lists)
    else:
        out = run([True] * chunks, tensors, lists)
    shaped = out.reshape(plane_tubes, local_frames, -1, heads, width)
    return jnp.swapaxes(shaped, 0, 1).reshape(queries.shape)


def solution(mesh):
    spec = P("st", "head", None, None)
    return jax.shard_map(
        body,
        mesh=mesh,
        in_specs=(spec, spec, spec, P("st", "head", None)),
        out_specs=spec,
        check_vma=False,
    )
```

```python
import functools

import jax
import jax.numpy as jnp
from jax import lax
from jax.experimental import pallas as pl
from jax.experimental.pallas import tpu as pltpu
from jax.sharding import PartitionSpec as P

BLK = 128


def pack_kernel(q_ref, k_ref, v_ref, out_ref):
    owners, _, held, rows, width = out_ref.shape
    for slot, ref in enumerate((q_ref, k_ref, v_ref)):
        turned = pltpu.einshape("phd->hpd", ref[...])
        out_ref[:, slot] = turned.reshape(owners, held, rows, width)


def pack(queries, key_vectors, value_vectors, first, tubes, rows, devs):
    heads, width = queries.shape[1:]
    held = tubes * heads // devs
    owners = heads // held
    step = min(rows, 32)
    steps = rows // step
    source = pl.BlockSpec((step, heads, width), lambda t, i: ((first + t) * steps + i, 0, 0))
    return pl.pallas_call(
        pack_kernel,
        out_shape=jax.ShapeDtypeStruct((devs, 3, held, rows, width), queries.dtype),
        grid=(tubes, steps),
        in_specs=[source, source, source],
        out_specs=pl.BlockSpec((owners, 3, held, step, width), lambda t, i: (t, 0, 0, i, 0)),
        cost_estimate=pl.CostEstimate(
            flops=0, transcendentals=0, bytes_accessed=12 * devs * held * rows * width
        ),
        name="pack",
    )(queries, key_vectors, value_vectors)


def unpack_kernel(src_ref, *refs):
    out_ref = refs[-1]
    owners, held, rows, width = src_ref.shape
    out_ref[...] = pltpu.einshape("hpd->phd", src_ref[...].reshape(owners * held, rows, width))


def unpack(arrived, out, first, tubes, all_rows):
    devs, held, rows, width = arrived.shape
    owners = devs // tubes
    heads = owners * held
    step = min(rows, 32)
    steps = rows // step
    operands, in_specs, aliases = [arrived], [], {}
    in_specs.append(pl.BlockSpec((owners, held, step, width), lambda t, i: (t, 0, i, 0)))
    if out is not None:
        operands.append(out)
        in_specs.append(pl.BlockSpec(memory_space=pl.ANY))
        aliases = {1: 0}
    return pl.pallas_call(
        unpack_kernel,
        out_shape=jax.ShapeDtypeStruct((all_rows, heads, width), arrived.dtype),
        grid=(tubes, steps),
        in_specs=in_specs,
        out_specs=pl.BlockSpec(
            (step, heads, width), lambda t, i: ((first + t) * steps + i, 0, 0)
        ),
        input_output_aliases=aliases,
        cost_estimate=pl.CostEstimate(
            flops=0, transcendentals=0, bytes_accessed=4 * devs * held * rows * width
        ),
        name="unpack",
    )(*operands)


def attend_kernel(tiles, per_group, base_ref, lists_ref, q_ref, k_ref, v_ref, o_ref):
    frames, rows, width = q_ref.shape
    tokens = frames * rows
    span = BLK // rows
    group = 2
    entries = tokens // BLK
    head = base_ref[1] + pl.program_id(0)
    stride = per_group * entries
    start = base_ref[0] + (head // per_group) * (tiles * stride) + (head % per_group) * entries
    keys = k_ref[...].reshape(tokens, width)
    values = v_ref[...].reshape(tokens, width)
    block_of = lax.broadcasted_iota(jnp.int32, (1, tokens), 1) // BLK
    scale = width ** (-0.5)
    for pair in range(tiles // group):
        query = q_ref[pair * group * span : (pair + 1) * group * span]
        query = query.reshape(group * BLK, width)
        scores = lax.dot_general(
            query, keys, (((1,), (1,)), ((), ())), preferred_element_type=jnp.float32
        )
        parts = []
        for member in range(group):
            tile = pair * group + member
            bits = jnp.int32(0)
            for e in range(entries):
                block = lists_ref[start + tile * stride + e]
                bits = bits | jnp.where(block >= 0, 1 << jnp.maximum(block, 0), 0)
            chosen = ((bits >> block_of) & 1) == 1
            bias = jnp.where(chosen, 0.0, -jnp.inf)
            part = scores[member * BLK : (member + 1) * BLK] * scale + bias
            weights = jnp.exp(part - jnp.max(part, axis=1, keepdims=True))
            total = jnp.sum(weights, axis=1, keepdims=True)
            parts.append((weights.astype(jnp.bfloat16), total))
        rounded = jnp.concatenate([part for part, _ in parts], axis=0)
        totals = jnp.concatenate([total for _, total in parts], axis=0)
        summed = jnp.dot(rounded, values, preferred_element_type=jnp.float32)
        result = (summed / totals).astype(o_ref.dtype)
        o_ref[pair * group * span : (pair + 1) * group * span] = result.reshape(
            group * span, rows, width
        )


def attend(arrived, base, lists, tiles, per_group):
    devs, _, held, rows, width = arrived.shape
    tokens = devs * rows

    def part(slot):
        return pl.BlockSpec((devs, None, None, rows, width), lambda u, *_: (0, slot, u, 0, 0))

    return pl.pallas_call(
        functools.partial(attend_kernel, tiles, per_group),
        out_shape=jax.ShapeDtypeStruct((devs, held, rows, width), arrived.dtype),
        grid_spec=pltpu.PrefetchScalarGridSpec(
            num_scalar_prefetch=2,
            grid=(held,),
            in_specs=[part(0), part(1), part(2)],
            out_specs=pl.BlockSpec((devs, None, rows, width), lambda u, *_: (0, u, 0, 0)),
        ),
        cost_estimate=pl.CostEstimate(
            flops=4 * held * tokens * tokens * width,
            transcendentals=held * tokens * tokens,
            bytes_accessed=8 * held * tokens * width,
        ),
        name="attend",
    )(base, lists, arrived, arrived, arrived)


def attend_own_kernel(q_ref, k_ref, v_ref, o_ref):
    owners, _, width = q_ref.shape
    scale = width ** (-0.5)
    heads = range(owners)
    scores = [
        lax.dot_general(
            q_ref[h], k_ref[h], (((1,), (1,)), ((), ())), preferred_element_type=jnp.float32
        )
        for h in heads
    ]
    weights, totals = [], []
    for h in heads:
        part = scores[h] * scale
        part = jnp.exp(part - jnp.max(part, axis=1, keepdims=True))
        totals.append(jnp.sum(part, axis=1, keepdims=True))
        weights.append(part.astype(jnp.bfloat16))
    for h in heads:
        summed = jnp.dot(weights[h], v_ref[h], preferred_element_type=jnp.float32)
        o_ref[h] = (summed / totals[h]).astype(o_ref.dtype)


def attend_own(packed):
    owners, _, held, rows, width = packed.shape

    def part(slot):
        return pl.BlockSpec((owners, None, None, rows, width), lambda u: (0, slot, u, 0, 0))

    return pl.pallas_call(
        attend_own_kernel,
        out_shape=jax.ShapeDtypeStruct((owners, held, rows, width), packed.dtype),
        grid=(held,),
        in_specs=[part(0), part(1), part(2)],
        out_specs=pl.BlockSpec((owners, None, rows, width), lambda u: (0, u, 0, 0)),
        cost_estimate=pl.CostEstimate(
            flops=4 * owners * held * rows * rows * width,
            transcendentals=owners * held * rows * rows,
            bytes_accessed=8 * owners * held * rows * width,
        ),
        name="attend_own",
    )(packed, packed, packed)


def exchange(blocks):
    return lax.all_to_all(blocks, "st", split_axis=0, concat_axis=0, tiled=True)


def body(queries, key_vectors, value_vectors, block_lists):
    head_devs = lax.axis_size("head")
    st_devs = lax.axis_size("st")
    local_frames, local_space, heads, width = queries.shape
    plane_tubes = st_devs // head_devs
    rows = local_frames * local_space // plane_tubes
    tiles, per_group, entries = block_lists.shape
    all_rows = local_frames * local_space
    chunk_tubes = 1 if heads % st_devs == 0 else plane_tubes
    held = chunk_tubes * heads // st_devs
    owners = st_devs // chunk_tubes
    chunks = plane_tubes // chunk_tubes

    def flat(source):
        shaped = source.reshape(local_frames, plane_tubes, -1, heads, width)
        return jnp.swapaxes(shaped, 0, 1).reshape(all_rows, heads, width)

    tensors = flat(queries), flat(key_vectors), flat(value_vectors)
    head_at, st_at = lax.axis_index("head"), lax.axis_index("st")
    tube_size = tiles * heads * entries
    mine = block_lists.reshape(-1, 128 if block_lists.size % 128 == 0 else entries)
    mine = lax.all_gather(mine, "head", axis=0, tiled=True)
    every = exchange(jnp.broadcast_to(mine, (st_devs, *mine.shape)))
    lists = lax.dynamic_slice_in_dim(every, head_at * plane_tubes, plane_tubes, 0)
    packed = [
        pack(*tensors, c * chunk_tubes, chunk_tubes, rows, st_devs) for c in range(chunks)
    ]

    def run(travels, packed, lists):
        out, arrived = None, {}
        for c in range(chunks):
            if travels[c]:
                arrived[c] = exchange(packed[c])
        for c in range(chunks):
            if not travels[c]:
                result = attend_own(packed[c])
                out = unpack(result, out, c * chunk_tubes, chunk_tubes, all_rows)
        for c, blocks in arrived.items():
            if out is not None and len(arrived) < chunks:
                blocks, out = lax.optimization_barrier((blocks, out))
            base = jnp.stack([(c + st_at // owners) * tube_size, (st_at % owners) * held])
            result = attend(blocks, base, lists, tiles, per_group)
            result = exchange(result)
            arrived[c] = result
        for c, result in arrived.items():
            out = unpack(result, out, c * chunk_tubes, chunk_tubes, all_rows)
        return out

    if rows == BLK and tiles == st_devs and chunk_tubes == 1 and plane_tubes <= 2:
        place = jnp.arange(tube_size) % (per_group * tiles * entries)
        tile_of = (place // (per_group * entries)).reshape(lists.shape[1:])[None]
        own = jnp.all((lists == tile_of) | (lists == -1), axis=(1, 2))
        which = jnp.sum(jnp.where(own, 0, 1 << jnp.arange(plane_tubes)))

        def branch(code):
            def go(packed, lists):
                return run([bool((code >> c) & 1) for c in range(chunks)], packed, lists)

            return go

        branches = [branch(code) for code in range(1 << chunks)]
        out = lax.switch(which, branches, packed, lists.reshape(-1))
    else:
        out = run([True] * chunks, packed, lists.reshape(-1))
    shaped = out.reshape(plane_tubes, local_frames, -1, heads, width)
    return jnp.swapaxes(shaped, 0, 1).reshape(queries.shape)


def solution(mesh):
    spec = P("st", "head", None, None)
    return jax.shard_map(
        body,
        mesh=mesh,
        in_specs=(spec, spec, spec, P("st", "head", None)),
        out_specs=spec,
        check_vma=False,
    )
```

```python
import functools

import jax
import jax.numpy as jnp
from jax import lax
from jax.experimental import pallas as pl
from jax.experimental.pallas import tpu as pltpu
from jax.sharding import PartitionSpec as P

BLK = 128


def pack_kernel(q_ref, k_ref, v_ref, out_ref):
    owners, _, held, rows, width = out_ref.shape
    for slot, ref in enumerate((k_ref, v_ref, q_ref)):
        turned = pltpu.einshape("phd->hpd", ref[...])
        out_ref[:, slot] = turned.reshape(owners, held, rows, width)


def pack(queries, key_vectors, value_vectors, first, tubes, rows, devs):
    heads, width = queries.shape[1:]
    held = tubes * heads // devs
    owners = heads // held
    step = min(rows, 32)
    steps = rows // step
    source = pl.BlockSpec((step, heads, width), lambda t, i: ((first + t) * steps + i, 0, 0))
    return pl.pallas_call(
        pack_kernel,
        out_shape=jax.ShapeDtypeStruct((devs, 3, held, rows, width), queries.dtype),
        grid=(tubes, steps),
        in_specs=[source, source, source],
        out_specs=pl.BlockSpec((owners, 3, held, step, width), lambda t, i: (t, 0, 0, i, 0)),
        cost_estimate=pl.CostEstimate(
            flops=0, transcendentals=0, bytes_accessed=12 * devs * held * rows * width
        ),
        name="pack",
    )(queries, key_vectors, value_vectors)


def unpack_kernel(src_ref, *refs):
    out_ref = refs[-1]
    owners, held, rows, width = src_ref.shape
    out_ref[...] = pltpu.einshape("hpd->phd", src_ref[...].reshape(owners * held, rows, width))


def unpack(arrived, out, first, tubes, all_rows):
    devs, held, rows, width = arrived.shape
    owners = devs // tubes
    heads = owners * held
    step = min(rows, 32)
    steps = rows // step
    operands, in_specs, aliases = [arrived], [], {}
    in_specs.append(pl.BlockSpec((owners, held, step, width), lambda t, i: (t, 0, i, 0)))
    if out is not None:
        operands.append(out)
        in_specs.append(pl.BlockSpec(memory_space=pl.ANY))
        aliases = {1: 0}
    return pl.pallas_call(
        unpack_kernel,
        out_shape=jax.ShapeDtypeStruct((all_rows, heads, width), arrived.dtype),
        grid=(tubes, steps),
        in_specs=in_specs,
        out_specs=pl.BlockSpec(
            (step, heads, width), lambda t, i: ((first + t) * steps + i, 0, 0)
        ),
        input_output_aliases=aliases,
        cost_estimate=pl.CostEstimate(
            flops=0, transcendentals=0, bytes_accessed=4 * devs * held * rows * width
        ),
        name="unpack",
    )(*operands)


def attend_kernel(tiles, per_group, base_ref, bits_ref, q_ref, k_ref, v_ref, o_ref):
    frames, rows, width = q_ref.shape
    tokens = frames * rows
    span = BLK // rows
    group = 2
    head = base_ref[1] + pl.program_id(0)
    start = base_ref[0] + (head // per_group) * (tiles * per_group) + head % per_group
    keys = k_ref[...].reshape(tokens, width)
    values = v_ref[...].reshape(tokens, width)
    block_of = lax.broadcasted_iota(jnp.int32, (1, tokens), 1) // BLK
    scale = width ** (-0.5)

    def step(pair, carry):
        here = pl.ds(pair * group * span, group * span)
        query = q_ref[here].reshape(group * BLK, width)
        scores = lax.dot_general(
            query, keys, (((1,), (1,)), ((), ())), preferred_element_type=jnp.float32
        )
        parts = []
        for member in range(group):
            tile = pair * group + member
            bits = bits_ref[start + tile * per_group]
            chosen = ((bits >> block_of) & 1) == 1
            bias = jnp.where(chosen, 0.0, -jnp.inf)
            part = scores[member * BLK : (member + 1) * BLK] * scale + bias
            weights = jnp.exp(part - jnp.max(part, axis=1, keepdims=True))
            total = jnp.sum(weights, axis=1, keepdims=True)
            parts.append((weights.astype(jnp.bfloat16), total))
        rounded = jnp.concatenate([part for part, _ in parts], axis=0)
        totals = jnp.concatenate([total for _, total in parts], axis=0)
        summed = jnp.dot(rounded, values, preferred_element_type=jnp.float32)
        result = (summed / totals).astype(o_ref.dtype)
        o_ref[here] = result.reshape(group * span, rows, width)
        return carry

    lax.fori_loop(0, tiles // group, step, 0)


def attend(arrived, base, bits, tiles, per_group):
    devs, _, held, rows, width = arrived.shape
    tokens = devs * rows

    def part(slot):
        return pl.BlockSpec((devs, None, None, rows, width), lambda u, *_: (0, slot, u, 0, 0))

    return pl.pallas_call(
        functools.partial(attend_kernel, tiles, per_group),
        out_shape=jax.ShapeDtypeStruct((devs, held, rows, width), arrived.dtype),
        grid_spec=pltpu.PrefetchScalarGridSpec(
            num_scalar_prefetch=2,
            grid=(held,),
            in_specs=[part(2), part(0), part(1)],
            out_specs=pl.BlockSpec((devs, None, rows, width), lambda u, *_: (0, u, 0, 0)),
        ),
        cost_estimate=pl.CostEstimate(
            flops=4 * held * tokens * tokens * width,
            transcendentals=held * tokens * tokens,
            bytes_accessed=8 * held * tokens * width,
        ),
        name="attend",
    )(base, bits, arrived, arrived, arrived)


def attend_own_kernel(q_ref, k_ref, v_ref, o_ref):
    owners, rows, width = q_ref.shape
    scale = width ** (-0.5)
    heads = range(owners)
    scores = [
        lax.dot_general(
            q_ref[h], k_ref[h], (((1,), (1,)), ((), ())), preferred_element_type=jnp.float32
        )
        for h in heads
    ]
    weights, totals = [], []
    for h in heads:
        part = scores[h] * scale
        part = jnp.exp(part - jnp.max(part, axis=1, keepdims=True))
        totals.append(jnp.sum(part, axis=1, keepdims=True))
        weights.append(part.astype(jnp.bfloat16))
    for h in heads:
        summed = jnp.dot(weights[h], v_ref[h], preferred_element_type=jnp.float32)
        o_ref[h] = (summed / totals[h]).astype(o_ref.dtype)


def attend_own(packed):
    owners, _, held, rows, width = packed.shape

    def part(slot):
        return pl.BlockSpec((owners, None, None, rows, width), lambda u: (0, slot, u, 0, 0))

    return pl.pallas_call(
        attend_own_kernel,
        out_shape=jax.ShapeDtypeStruct((owners, held, rows, width), packed.dtype),
        grid=(held,),
        in_specs=[part(2), part(0), part(1)],
        out_specs=pl.BlockSpec((owners, None, rows, width), lambda u: (0, u, 0, 0)),
        cost_estimate=pl.CostEstimate(
            flops=4 * owners * held * rows * rows * width,
            transcendentals=owners * held * rows * rows,
            bytes_accessed=8 * owners * held * rows * width,
        ),
        name="attend_own",
    )(packed, packed, packed)


def gather_kernel(tiles, per_group, tubes, me_ref, bits_ref, *refs):
    sources, out_ref = refs[:-1], refs[-1]
    owners, _, held, _, _ = sources[0].shape
    me, there = me_ref[0], pl.program_id(0)
    count = jnp.int32(0)
    for tube, source in zip(tubes, sources):

        def step(u, count, tube=tube, source=source):
            for owner in range(owners):
                head = owner * held
                place = (tube * owners * held + head // per_group * per_group) * tiles
                bits = bits_ref[place + there * per_group + head % per_group + u]
                chosen = jnp.where(there == me, 0, (bits >> me) & 1)

                @pl.when(chosen == 1)
                def _(count=count, owner=owner):
                    out_ref[count] = source[owner, :, u]

                count = count + chosen
            return count

        count = lax.fori_loop(0, held, step, count)


def gather(me, bits, packed, tubes, cap, tiles, per_group):
    owners, _, held, rows, width = packed[tubes[0]].shape
    source = pl.BlockSpec((owners, 2, held, rows, width), lambda f, *_: (0, 0, 0, 0, 0))
    return pl.pallas_call(
        functools.partial(gather_kernel, tiles, per_group, tubes),
        out_shape=jax.ShapeDtypeStruct((owners, cap, 2, rows, width), packed[0].dtype),
        grid_spec=pltpu.PrefetchScalarGridSpec(
            num_scalar_prefetch=2,
            grid=(owners,),
            in_specs=[source] * len(tubes),
            out_specs=pl.BlockSpec((None, cap, 2, rows, width), lambda f, *_: (f, 0, 0, 0, 0)),
        ),
        cost_estimate=pl.CostEstimate(
            flops=0, transcendentals=0, bytes_accessed=8 * owners * cap * rows * width
        ),
        name="gather",
    )(me, bits, *[packed[c] for c in tubes])


def attend_few_kernel(
    tiles, per_group, tube, me_ref, bits_ref, start_ref, q_ref, k_ref, v_ref, far_ref,
    o_ref, count_ref, slot_ref, keys_ref, values_ref,
):
    owners, rows, width = q_ref.shape
    blocks = far_ref.shape[0]
    held = pl.num_programs(0)
    u, me = pl.program_id(0), me_ref[0]
    scale = width ** (-0.5)

    @pl.when(u == 0)
    def _():
        for b in range(blocks):
            count_ref[b] = start_ref[b]

    def word(owner):
        head = owner * held
        place = (tube * owners * held + head // per_group * per_group) * tiles
        return bits_ref[place + me * per_group + head % per_group + u]

    counts = [count_ref[b] for b in range(blocks)]
    most, pick = jnp.int32(0), []
    for owner in range(owners):
        bits = word(owner)
        number, at, slot = jnp.int32(0), jnp.int32(0), jnp.int32(0)
        for b in range(blocks):
            chosen = jnp.where(me == b, 0, (bits >> b) & 1)
            slot_ref[owner * blocks + b] = counts[b]
            at = jnp.where(chosen == 1, b, at)
            slot = jnp.where(chosen == 1, counts[b], slot)
            counts[b] = counts[b] + chosen
            number = number + chosen
        most = jnp.maximum(most, number)
        pick.append((number, at, slot))
        bits_of = bits
        slot_ref[owners * blocks + owner] = bits_of
    for b in range(blocks):
        count_ref[b] = counts[b]

    def normal(scores):
        weights = jnp.exp(scores - jnp.max(scores, axis=1, keepdims=True))
        total = jnp.sum(weights, axis=1, keepdims=True)
        return weights.astype(jnp.bfloat16), total

    @pl.when(most <= 1)
    def _():
        lane = lax.broadcasted_iota(jnp.int32, (1, 2 * rows), 1)
        scores, values = [], []
        for owner, (number, at, slot) in enumerate(pick):
            far = number == 1
            key, value = k_ref[owner], v_ref[owner]
            keys = jnp.concatenate([key, jnp.where(far, far_ref[at, slot, 0], key)], axis=0)
            values.append(
                jnp.concatenate([value, jnp.where(far, far_ref[at, slot, 1], value)], axis=0)
            )
            part = lax.dot_general(
                q_ref[owner], keys, (((1,), (1,)), ((), ())), preferred_element_type=jnp.float32
            )
            bias = jnp.where(lane < rows + rows * number, 0.0, -jnp.inf)
            scores.append(part * scale + bias)
        parts = [normal(part) for part in scores]
        for owner, (weights, total) in enumerate(parts):
            summed = jnp.dot(weights, values[owner], preferred_element_type=jnp.float32)
            o_ref[owner] = (summed / total).astype(o_ref.dtype)

    @pl.when(most > 1)
    def _():
        block_of = lax.broadcasted_iota(jnp.int32, (1, blocks * rows), 1) // rows

        def one(owner, carry):
            bits = slot_ref[owners * blocks + owner]
            for b in range(blocks):
                far = jnp.where(me == b, 0, (bits >> b) & 1) == 1
                here = slice(b * rows, (b + 1) * rows)

                @pl.when(far)
                def _(b=b, here=here):
                    slot = slot_ref[owner * blocks + b]
                    keys_ref[here] = far_ref[b, slot, 0]
                    values_ref[here] = far_ref[b, slot, 1]

                @pl.when(jnp.logical_not(far))
                def _(here=here):
                    keys_ref[here] = k_ref[owner]
                    values_ref[here] = v_ref[owner]

            bias = jnp.where(((bits >> block_of) & 1) == 1, 0.0, -jnp.inf)
            part = lax.dot_general(
                q_ref[owner],
                keys_ref[...],
                (((1,), (1,)), ((), ())),
                preferred_element_type=jnp.float32,
            )
            weights, total = normal(part * scale + bias)
            summed = jnp.dot(weights, values_ref[...], preferred_element_type=jnp.float32)
            o_ref[owner] = (summed / total).astype(o_ref.dtype)
            return carry

        lax.fori_loop(0, owners, one, 0)


def attend_few(me, bits, start, packed, far, tube, tiles, per_group):
    owners, _, held, rows, width = packed.shape
    blocks, cap = far.shape[:2]

    def part(slot):
        return pl.BlockSpec((owners, None, None, rows, width), lambda u, *_: (0, slot, u, 0, 0))

    return pl.pallas_call(
        functools.partial(attend_few_kernel, tiles, per_group, tube),
        out_shape=jax.ShapeDtypeStruct((owners, held, rows, width), packed.dtype),
        grid_spec=pltpu.PrefetchScalarGridSpec(
            num_scalar_prefetch=3,
            grid=(held,),
            in_specs=[
                part(2),
                part(0),
                part(1),
                pl.BlockSpec(far.shape, lambda u, *_: (0, 0, 0, 0, 0)),
            ],
            out_specs=pl.BlockSpec((owners, None, rows, width), lambda u, *_: (0, u, 0, 0)),
            scratch_shapes=[
                pltpu.SMEM((blocks,), jnp.int32),
                pltpu.SMEM((owners * (blocks + 1),), jnp.int32),
                pltpu.VMEM((blocks * rows, width), packed.dtype),
                pltpu.VMEM((blocks * rows, width), packed.dtype),
            ],
        ),
        cost_estimate=pl.CostEstimate(
            flops=8 * owners * held * rows * rows * width,
            transcendentals=2 * owners * held * rows * rows,
            bytes_accessed=8 * owners * held * rows * width + 4 * blocks * cap * rows * width,
        ),
        name="attend_few",
    )(me, bits, start, packed, packed, packed, far)


def exchange(blocks):
    return lax.all_to_all(blocks, "st", split_axis=0, concat_axis=0, tiled=True)


def body(queries, key_vectors, value_vectors, block_lists):
    head_devs = lax.axis_size("head")
    st_devs = lax.axis_size("st")
    local_frames, local_space, heads, width = queries.shape
    plane_tubes = st_devs // head_devs
    rows = local_frames * local_space // plane_tubes
    tiles, per_group, entries = block_lists.shape
    all_rows = local_frames * local_space
    chunk_tubes = 1 if heads % st_devs == 0 else plane_tubes
    held = chunk_tubes * heads // st_devs
    owners = st_devs // chunk_tubes
    chunks = plane_tubes // chunk_tubes

    def flat(source):
        shaped = source.reshape(local_frames, plane_tubes, -1, heads, width)
        return jnp.swapaxes(shaped, 0, 1).reshape(all_rows, heads, width)

    tensors = flat(queries), flat(key_vectors), flat(value_vectors)
    head_at, st_at = lax.axis_index("head"), lax.axis_index("st")
    tube_size = tiles * heads * entries
    mine = block_lists.reshape(-1, 128 if block_lists.size % 128 == 0 else entries)
    mine = lax.all_gather(mine, "head", axis=0, tiled=True)
    every = exchange(jnp.broadcast_to(mine, (st_devs, *mine.shape)))
    lists = lax.dynamic_slice_in_dim(every, head_at * plane_tubes, plane_tubes, 0)
    tile_size = tiles * heads
    values = jnp.where(lists >= 0, 1 << jnp.maximum(lists, 0), 0).astype(jnp.float32)
    lanes = lists.shape[-1]
    joins = jnp.arange(lanes)[:, None] // entries == jnp.arange(lanes // entries)[None]
    bits = jnp.dot(
        values.reshape(-1, lanes), joins.astype(jnp.float32), precision=lax.Precision.HIGHEST
    )
    bits = bits.astype(jnp.int32).reshape(-1)
    packed = [
        pack(*tensors, c * chunk_tubes, chunk_tubes, rows, st_devs) for c in range(chunks)
    ]
    me = jnp.stack([st_at])

    def run(whole, few, cap, packed, bits, counts):
        out, arrived, far = None, {}, None
        for c in whole:
            arrived[c] = exchange(packed[c])
        if few:
            far = exchange(gather(me, bits, packed, few, cap, tiles, per_group))
        for c in range(chunks):
            if c not in whole and c not in few:
                result = attend_own(packed[c])
                out = unpack(result, out, c * chunk_tubes, chunk_tubes, all_rows)
        for c in whole:
            blocks = arrived[c]
            if out is not None and len(whole) < chunks:
                blocks, out = lax.optimization_barrier((blocks, out))
            base = jnp.stack([(c + st_at // owners) * tile_size, (st_at % owners) * held])
            arrived[c] = exchange(attend(blocks, base, bits, tiles, per_group))
        start = jnp.zeros_like(counts[0])
        for c in few:
            result = attend_few(me, bits, start, packed[c], far, c, tiles, per_group)
            start = start + counts[c]
            out = unpack(result, out, c * chunk_tubes, chunk_tubes, all_rows)
        for c in whole:
            out = unpack(arrived[c], out, c * chunk_tubes, chunk_tubes, all_rows)
        return out

    few_possible = rows == BLK and tiles == st_devs and chunk_tubes == 1
    if few_possible and plane_tubes == 2 and per_group % held == 0:
        place = jnp.arange(tube_size) % (per_group * tiles * entries)
        tile_of = (place // (per_group * entries)).reshape(lists.shape[1:])
        hits = lists[:, None] == jnp.arange(tiles)[None, :, None, None]
        spread = tile_of[..., None] == jnp.arange(tiles)
        need = jnp.einsum(
            "cbrl,rlt->cbt",
            hits.astype(jnp.bfloat16),
            spread.astype(jnp.bfloat16),
            preferred_element_type=jnp.float32,
        )
        need = jnp.where(jnp.eye(tiles, dtype=bool)[None], 0.0, need)
        counts = jnp.sum(jnp.where(jnp.arange(tiles) == st_at, need, 0.0), axis=2)
        counts = counts.astype(jnp.int32)
        most_a, most_b = jnp.max(need[0]), jnp.max(need[1])
        both = jnp.max(need[0] + need[1])
        one_cap, two_cap = heads // 5, heads // 3
        a = jnp.where(most_a == 0, 0, jnp.where(most_a <= one_cap, 1, 2))
        b = jnp.where(most_b == 0, 0, jnp.where(most_b <= one_cap, 1, 2))
        pair = (a > 0) & (b > 0) & (both <= two_cap)
        a = jnp.where((a == 1) & (b == 1), 2, a)
        which = jnp.where(pair, 4, a * 3 + b)
        plans = [
            ((), (), 0),
            ((), (1,), one_cap),
            ((1,), (), 0),
            ((), (0,), one_cap),
            ((), (0, 1), two_cap),
            ((1,), (0,), one_cap),
            ((0,), (), 0),
            ((0,), (1,), one_cap),
            ((0, 1), (), 0),
        ]

        def branch(plan):
            return lambda packed, bits, counts: run(*plan, packed, bits, counts)

        out = lax.switch(which, [branch(plan) for plan in plans], packed, bits, counts)
    else:
        none = [jnp.zeros((tiles,), jnp.int32)]
        out = run(tuple(range(chunks)), (), 0, packed, bits, none)
    shaped = out.reshape(plane_tubes, local_frames, -1, heads, width)
    return jnp.swapaxes(shaped, 0, 1).reshape(queries.shape)


def solution(mesh):
    spec = P("st", "head", None, None)
    return jax.shard_map(
        body,
        mesh=mesh,
        in_specs=(spec, spec, spec, P("st", "head", None)),
        out_specs=spec,
        check_vma=False,
    )
```

```python
import functools

import jax
import jax.numpy as jnp
from jax import lax
from jax.experimental import pallas as pl
from jax.experimental.pallas import tpu as pltpu
from jax.sharding import PartitionSpec as P

BLK = 128


def pack_kernel(q_ref, k_ref, v_ref, out_ref):
    owners, _, held, rows, width = out_ref.shape
    for slot, ref in enumerate((k_ref, v_ref, q_ref)):
        turned = pltpu.einshape("phd->hpd", ref[...])
        out_ref[:, slot] = turned.reshape(owners, held, rows, width)


def pack(queries, key_vectors, value_vectors, first, tubes, rows, devs):
    heads, width = queries.shape[1:]
    held = tubes * heads // devs
    owners = heads // held
    step = min(rows, 32)
    steps = rows // step
    source = pl.BlockSpec((step, heads, width), lambda t, i: ((first + t) * steps + i, 0, 0))
    return pl.pallas_call(
        pack_kernel,
        out_shape=jax.ShapeDtypeStruct((devs, 3, held, rows, width), queries.dtype),
        grid=(tubes, steps),
        in_specs=[source, source, source],
        out_specs=pl.BlockSpec((owners, 3, held, step, width), lambda t, i: (t, 0, 0, i, 0)),
        cost_estimate=pl.CostEstimate(
            flops=0, transcendentals=0, bytes_accessed=12 * devs * held * rows * width
        ),
        name="pack",
    )(queries, key_vectors, value_vectors)


def unpack_kernel(src_ref, *refs):
    out_ref = refs[-1]
    owners, held, rows, width = src_ref.shape
    out_ref[...] = pltpu.einshape("hpd->phd", src_ref[...].reshape(owners * held, rows, width))


def unpack(arrived, out, first, tubes, all_rows):
    devs, held, rows, width = arrived.shape
    owners = devs // tubes
    heads = owners * held
    step = min(rows, 32)
    steps = rows // step
    operands, in_specs, aliases = [arrived], [], {}
    in_specs.append(pl.BlockSpec((owners, held, step, width), lambda t, i: (t, 0, i, 0)))
    if out is not None:
        operands.append(out)
        in_specs.append(pl.BlockSpec(memory_space=pl.ANY))
        aliases = {1: 0}
    return pl.pallas_call(
        unpack_kernel,
        out_shape=jax.ShapeDtypeStruct((all_rows, heads, width), arrived.dtype),
        grid=(tubes, steps),
        in_specs=in_specs,
        out_specs=pl.BlockSpec(
            (step, heads, width), lambda t, i: ((first + t) * steps + i, 0, 0)
        ),
        input_output_aliases=aliases,
        cost_estimate=pl.CostEstimate(
            flops=0, transcendentals=0, bytes_accessed=4 * devs * held * rows * width
        ),
        name="unpack",
    )(*operands)


def attend_kernel(tiles, per_group, plane_tubes, unroll, base_ref, bits_ref, q_ref, k_ref, v_ref, o_ref):
    frames, rows, width = q_ref.shape
    tokens = frames * rows
    span = BLK // rows
    group = 2
    head = base_ref[1] + pl.program_id(0)
    group_tube = head // per_group * plane_tubes + base_ref[0]
    start = group_tube * tiles * per_group + head % per_group
    keys = k_ref[...].reshape(tokens, width)
    values = v_ref[...].reshape(tokens, width)
    block_of = lax.broadcasted_iota(jnp.int32, (1, tokens), 1) // BLK
    scale = width ** (-0.5)

    def step(pair, carry):
        here = pl.ds(pair * group * span, group * span)
        query = q_ref[here].reshape(group * BLK, width)
        scores = lax.dot_general(
            query, keys, (((1,), (1,)), ((), ())), preferred_element_type=jnp.float32
        )
        parts = []
        for member in range(group):
            tile = pair * group + member
            bits = bits_ref[start + tile * per_group]
            chosen = ((bits >> block_of) & 1) == 1
            bias = jnp.where(chosen, 0.0, -jnp.inf)
            part = scores[member * BLK : (member + 1) * BLK] * scale + bias
            weights = jnp.exp(part - jnp.max(part, axis=1, keepdims=True))
            total = jnp.sum(weights, axis=1, keepdims=True)
            parts.append((weights.astype(jnp.bfloat16), total))
        rounded = jnp.concatenate([part for part, _ in parts], axis=0)
        totals = jnp.concatenate([total for _, total in parts], axis=0)
        summed = jnp.dot(rounded, values, preferred_element_type=jnp.float32)
        result = (summed / totals).astype(o_ref.dtype)
        o_ref[here] = result.reshape(group * span, rows, width)
        return carry

    if unroll:
        for pair in range(tiles // group):
            step(pair, 0)
    else:
        lax.fori_loop(0, tiles // group, step, 0)


def attend(arrived, base, bits, tiles, per_group, plane_tubes, unroll):
    devs, _, held, rows, width = arrived.shape
    tokens = devs * rows

    def part(slot):
        return pl.BlockSpec((devs, None, None, rows, width), lambda u, *_: (0, slot, u, 0, 0))

    return pl.pallas_call(
        functools.partial(attend_kernel, tiles, per_group, plane_tubes, unroll),
        out_shape=jax.ShapeDtypeStruct((devs, held, rows, width), arrived.dtype),
        grid_spec=pltpu.PrefetchScalarGridSpec(
            num_scalar_prefetch=2,
            grid=(held,),
            in_specs=[part(2), part(0), part(1)],
            out_specs=pl.BlockSpec((devs, None, rows, width), lambda u, *_: (0, u, 0, 0)),
        ),
        cost_estimate=pl.CostEstimate(
            flops=4 * held * tokens * tokens * width,
            transcendentals=held * tokens * tokens,
            bytes_accessed=8 * held * tokens * width,
        ),
        name="attend",
    )(base, bits, arrived, arrived, arrived)


def attend_own_kernel(q_ref, k_ref, v_ref, o_ref):
    owners, rows, width = q_ref.shape
    scale = width ** (-0.5)
    heads = range(owners)
    scores = [
        lax.dot_general(
            q_ref[h], k_ref[h], (((1,), (1,)), ((), ())), preferred_element_type=jnp.float32
        )
        for h in heads
    ]
    weights, totals = [], []
    for h in heads:
        part = scores[h] * scale
        part = jnp.exp(part - jnp.max(part, axis=1, keepdims=True))
        totals.append(jnp.sum(part, axis=1, keepdims=True))
        weights.append(part.astype(jnp.bfloat16))
    for h in heads:
        summed = jnp.dot(weights[h], v_ref[h], preferred_element_type=jnp.float32)
        o_ref[h] = (summed / totals[h]).astype(o_ref.dtype)


def attend_own(packed):
    owners, _, held, rows, width = packed.shape

    def part(slot):
        return pl.BlockSpec((owners, None, None, rows, width), lambda u: (0, slot, u, 0, 0))

    return pl.pallas_call(
        attend_own_kernel,
        out_shape=jax.ShapeDtypeStruct((owners, held, rows, width), packed.dtype),
        grid=(held,),
        in_specs=[part(2), part(0), part(1)],
        out_specs=pl.BlockSpec((owners, None, rows, width), lambda u: (0, u, 0, 0)),
        cost_estimate=pl.CostEstimate(
            flops=4 * owners * held * rows * rows * width,
            transcendentals=owners * held * rows * rows,
            bytes_accessed=8 * owners * held * rows * width,
        ),
        name="attend_own",
    )(packed, packed, packed)


def gather_kernel(tiles, per_group, plane_tubes, tubes, me_ref, bits_ref, *refs):
    sources, out_ref = refs[:-1], refs[-1]
    owners, _, held, _, _ = sources[0].shape
    me, there = me_ref[0], pl.program_id(0)
    count = jnp.int32(0)
    for tube, source in zip(tubes, sources):

        def step(u, count, tube=tube, source=source):
            for owner in range(owners):
                head = owner * held
                place = (head // per_group * plane_tubes + tube) * tiles * per_group
                bits = bits_ref[place + there * per_group + head % per_group + u]
                chosen = jnp.where(there == me, 0, (bits >> me) & 1)

                @pl.when(chosen == 1)
                def _(count=count, owner=owner):
                    out_ref[count] = source[owner, :, u]

                count = count + chosen
            return count

        count = lax.fori_loop(0, held, step, count)


def gather(me, bits, packed, tubes, cap, tiles, per_group, plane_tubes):
    owners, _, held, rows, width = packed[tubes[0]].shape
    source = pl.BlockSpec((owners, 2, held, rows, width), lambda f, *_: (0, 0, 0, 0, 0))
    return pl.pallas_call(
        functools.partial(gather_kernel, tiles, per_group, plane_tubes, tubes),
        out_shape=jax.ShapeDtypeStruct((owners, cap, 2, rows, width), packed[0].dtype),
        grid_spec=pltpu.PrefetchScalarGridSpec(
            num_scalar_prefetch=2,
            grid=(owners,),
            in_specs=[source] * len(tubes),
            out_specs=pl.BlockSpec((None, cap, 2, rows, width), lambda f, *_: (f, 0, 0, 0, 0)),
        ),
        cost_estimate=pl.CostEstimate(
            flops=0, transcendentals=0, bytes_accessed=8 * owners * cap * rows * width
        ),
        name="gather",
    )(me, bits, *[packed[c] for c in tubes])


def attend_few_kernel(
    tiles, per_group, plane_tubes, tube, me_ref, bits_ref, start_ref, q_ref, k_ref, v_ref, far_ref,
    o_ref, count_ref, slot_ref, keys_ref, values_ref,
):
    owners, rows, width = q_ref.shape
    blocks = far_ref.shape[0]
    held = pl.num_programs(0)
    u, me = pl.program_id(0), me_ref[0]
    scale = width ** (-0.5)

    @pl.when(u == 0)
    def _():
        for b in range(blocks):
            count_ref[b] = start_ref[b]

    def word(owner):
        head = owner * held
        place = (head // per_group * plane_tubes + tube) * tiles * per_group
        return bits_ref[place + me * per_group + head % per_group + u]

    counts = [count_ref[b] for b in range(blocks)]
    most, pick = jnp.int32(0), []
    for owner in range(owners):
        bits = word(owner)
        number, at, slot = jnp.int32(0), jnp.int32(0), jnp.int32(0)
        for b in range(blocks):
            chosen = jnp.where(me == b, 0, (bits >> b) & 1)
            slot_ref[owner * blocks + b] = counts[b]
            at = jnp.where(chosen == 1, b, at)
            slot = jnp.where(chosen == 1, counts[b], slot)
            counts[b] = counts[b] + chosen
            number = number + chosen
        most = jnp.maximum(most, number)
        pick.append((number, at, slot))
        bits_of = bits
        slot_ref[owners * blocks + owner] = bits_of
    for b in range(blocks):
        count_ref[b] = counts[b]

    def normal(scores):
        weights = jnp.exp(scores - jnp.max(scores, axis=1, keepdims=True))
        total = jnp.sum(weights, axis=1, keepdims=True)
        return weights.astype(jnp.bfloat16), total

    @pl.when(most <= 1)
    def _():
        lane = lax.broadcasted_iota(jnp.int32, (1, 2 * rows), 1)
        scores, values = [], []
        for owner, (number, at, slot) in enumerate(pick):
            far = number == 1
            key, value = k_ref[owner], v_ref[owner]
            keys = jnp.concatenate([key, jnp.where(far, far_ref[at, slot, 0], key)], axis=0)
            values.append(
                jnp.concatenate([value, jnp.where(far, far_ref[at, slot, 1], value)], axis=0)
            )
            part = lax.dot_general(
                q_ref[owner], keys, (((1,), (1,)), ((), ())), preferred_element_type=jnp.float32
            )
            bias = jnp.where(lane < rows + rows * number, 0.0, -jnp.inf)
            scores.append(part * scale + bias)
        parts = [normal(part) for part in scores]
        for owner, (weights, total) in enumerate(parts):
            summed = jnp.dot(weights, values[owner], preferred_element_type=jnp.float32)
            o_ref[owner] = (summed / total).astype(o_ref.dtype)

    @pl.when(most > 1)
    def _():
        block_of = lax.broadcasted_iota(jnp.int32, (1, blocks * rows), 1) // rows

        def one(owner, carry):
            bits = slot_ref[owners * blocks + owner]
            for b in range(blocks):
                far = jnp.where(me == b, 0, (bits >> b) & 1) == 1
                here = slice(b * rows, (b + 1) * rows)

                @pl.when(far)
                def _(b=b, here=here):
                    slot = slot_ref[owner * blocks + b]
                    keys_ref[here] = far_ref[b, slot, 0]
                    values_ref[here] = far_ref[b, slot, 1]

                @pl.when(jnp.logical_not(far))
                def _(here=here):
                    keys_ref[here] = k_ref[owner]
                    values_ref[here] = v_ref[owner]

            bias = jnp.where(((bits >> block_of) & 1) == 1, 0.0, -jnp.inf)
            part = lax.dot_general(
                q_ref[owner],
                keys_ref[...],
                (((1,), (1,)), ((), ())),
                preferred_element_type=jnp.float32,
            )
            weights, total = normal(part * scale + bias)
            summed = jnp.dot(weights, values_ref[...], preferred_element_type=jnp.float32)
            o_ref[owner] = (summed / total).astype(o_ref.dtype)
            return carry

        lax.fori_loop(0, owners, one, 0)


def attend_few(me, bits, start, packed, far, tube, tiles, per_group, plane_tubes):
    owners, _, held, rows, width = packed.shape
    blocks, cap = far.shape[:2]

    def part(slot):
        return pl.BlockSpec((owners, None, None, rows, width), lambda u, *_: (0, slot, u, 0, 0))

    return pl.pallas_call(
        functools.partial(attend_few_kernel, tiles, per_group, plane_tubes, tube),
        out_shape=jax.ShapeDtypeStruct((owners, held, rows, width), packed.dtype),
        grid_spec=pltpu.PrefetchScalarGridSpec(
            num_scalar_prefetch=3,
            grid=(held,),
            in_specs=[
                part(2),
                part(0),
                part(1),
                pl.BlockSpec(far.shape, lambda u, *_: (0, 0, 0, 0, 0)),
            ],
            out_specs=pl.BlockSpec((owners, None, rows, width), lambda u, *_: (0, u, 0, 0)),
            scratch_shapes=[
                pltpu.SMEM((blocks,), jnp.int32),
                pltpu.SMEM((owners * (blocks + 1),), jnp.int32),
                pltpu.VMEM((blocks * rows, width), packed.dtype),
                pltpu.VMEM((blocks * rows, width), packed.dtype),
            ],
        ),
        cost_estimate=pl.CostEstimate(
            flops=8 * owners * held * rows * rows * width,
            transcendentals=2 * owners * held * rows * rows,
            bytes_accessed=8 * owners * held * rows * width + 4 * blocks * cap * rows * width,
        ),
        name="attend_few",
    )(me, bits, start, packed, packed, packed, far)


def exchange(blocks):
    return lax.all_to_all(blocks, "st", split_axis=0, concat_axis=0, tiled=True)


def body(queries, key_vectors, value_vectors, block_lists):
    head_devs = lax.axis_size("head")
    st_devs = lax.axis_size("st")
    local_frames, local_space, heads, width = queries.shape
    plane_tubes = st_devs // head_devs
    rows = local_frames * local_space // plane_tubes
    tiles, per_group, entries = block_lists.shape
    all_rows = local_frames * local_space
    chunk_tubes = 1 if heads % st_devs == 0 else plane_tubes
    held = chunk_tubes * heads // st_devs
    owners = st_devs // chunk_tubes
    chunks = plane_tubes // chunk_tubes

    def flat(source):
        shaped = source.reshape(local_frames, plane_tubes, -1, heads, width)
        return jnp.swapaxes(shaped, 0, 1).reshape(all_rows, heads, width)

    tensors = flat(queries), flat(key_vectors), flat(value_vectors)
    head_at, st_at = lax.axis_index("head"), lax.axis_index("st")
    tile_size = tiles * per_group
    mine = jnp.broadcast_to(block_lists.reshape(1, 1, -1), (head_devs * st_devs, 1, block_lists.size))
    every = lax.all_to_all(mine, ("head", "st"), split_axis=0, concat_axis=0, tiled=True)
    every = every.reshape(head_devs, st_devs, block_lists.size)
    lists = lax.dynamic_slice_in_dim(every, head_at * plane_tubes, plane_tubes, 1)
    values = jnp.where(lists >= 0, 1 << jnp.maximum(lists, 0), 0).astype(jnp.float32)
    words = tile_size
    joins = jnp.arange(words * entries)[:, None] // entries == jnp.arange(words)[None]
    bits = jnp.dot(
        values.reshape(-1, words * entries),
        joins.astype(jnp.float32),
        precision=lax.Precision.HIGHEST,
    )
    bits = bits.astype(jnp.int32).reshape(-1)
    packed = [
        pack(*tensors, c * chunk_tubes, chunk_tubes, rows, st_devs) for c in range(chunks)
    ]
    me = jnp.stack([st_at])

    def run(whole, few, cap, packed, bits, counts):
        out, arrived, far = None, {}, None
        for c in whole:
            arrived[c] = exchange(packed[c])
        if few:
            far = exchange(gather(me, bits, packed, few, cap, tiles, per_group, plane_tubes))
        for c in range(chunks):
            if c not in whole and c not in few:
                result = attend_own(packed[c])
                out = unpack(result, out, c * chunk_tubes, chunk_tubes, all_rows)
        for c in whole:
            blocks = arrived[c]
            if out is not None and len(whole) < chunks:
                blocks, out = lax.optimization_barrier((blocks, out))
            base = jnp.stack([c + st_at // owners, (st_at % owners) * held])
            alone = len(whole) == 1 and not few
            result = attend(blocks, base, bits, tiles, per_group, plane_tubes, alone)
            arrived[c] = exchange(result)
        start = jnp.zeros_like(counts[0])
        for c in few:
            result = attend_few(me, bits, start, packed[c], far, c, tiles, per_group, plane_tubes)
            start = start + counts[c]
            out = unpack(result, out, c * chunk_tubes, chunk_tubes, all_rows)
        for c in whole:
            out = unpack(arrived[c], out, c * chunk_tubes, chunk_tubes, all_rows)
        return out

    few_possible = rows == BLK and tiles == st_devs and chunk_tubes == 1
    if few_possible and plane_tubes == 2 and per_group % held == 0:
        tile_of = jnp.arange(words * entries) // (per_group * entries)
        hits = lists[:, :, None] == jnp.arange(tiles)[None, None, :, None]
        spread = tile_of[:, None] == jnp.arange(tiles)
        need = jnp.einsum(
            "gcbl,lt->cbt",
            hits.astype(jnp.bfloat16),
            spread.astype(jnp.bfloat16),
            preferred_element_type=jnp.float32,
        )
        need = jnp.where(jnp.eye(tiles, dtype=bool)[None], 0.0, need)
        counts = jnp.sum(jnp.where(jnp.arange(tiles) == st_at, need, 0.0), axis=2)
        counts = counts.astype(jnp.int32)
        one_cap, two_cap = heads // 5, heads // 3
        most = jnp.max(jnp.concatenate([need, need[:1] + need[1:]]), axis=(1, 2))
        bound = jnp.where(jnp.arange(3) == 2, two_cap, one_cap)
        level = jnp.where(most == 0, 0, jnp.where(most <= bound, 1, 2))
        code = jnp.sum(level << (2 * jnp.arange(3)))
        a, b, both = code & 3, (code >> 2) & 3, code >> 4
        pair = (a > 0) & (b > 0) & (both <= 1)
        a = jnp.where((a == 1) & (b == 1), 2, a)
        which = jnp.where(pair, 4, a * 3 + b)
        plans = [
            ((), (), 0),
            ((), (1,), one_cap),
            ((1,), (), 0),
            ((), (0,), one_cap),
            ((), (0, 1), two_cap),
            ((1,), (0,), one_cap),
            ((0,), (), 0),
            ((0,), (1,), one_cap),
            ((0, 1), (), 0),
        ]

        def branch(plan):
            return lambda packed, bits, counts: run(*plan, packed, bits, counts)

        out = lax.switch(which, [branch(plan) for plan in plans], packed, bits, counts)
    else:
        none = [jnp.zeros((tiles,), jnp.int32)]
        out = run(tuple(range(chunks)), (), 0, packed, bits, none)
    shaped = out.reshape(plane_tubes, local_frames, -1, heads, width)
    return jnp.swapaxes(shaped, 0, 1).reshape(queries.shape)


def solution(mesh):
    spec = P("st", "head", None, None)
    return jax.shard_map(
        body,
        mesh=mesh,
        in_specs=(spec, spec, spec, P("st", "head", None)),
        out_specs=spec,
        check_vma=False,
    )
```

```python
import functools

import jax
import jax.numpy as jnp
from jax import lax
from jax.experimental import pallas as pl
from jax.experimental.pallas import tpu as pltpu
from jax.sharding import PartitionSpec as P

BLK = 128


def pack_kernel(q_ref, k_ref, v_ref, out_ref):
    owners, _, held, rows, width = out_ref.shape
    for slot, ref in enumerate((k_ref, v_ref, q_ref)):
        turned = pltpu.einshape("phd->hpd", ref[...])
        out_ref[:, slot] = turned.reshape(owners, held, rows, width)


def pack(queries, key_vectors, value_vectors, first, tubes, rows, devs):
    heads, width = queries.shape[1:]
    held = tubes * heads // devs
    owners = heads // held
    step = min(rows, 64)
    steps = rows // step
    source = pl.BlockSpec((step, heads, width), lambda t, i: ((first + t) * steps + i, 0, 0))
    return pl.pallas_call(
        pack_kernel,
        out_shape=jax.ShapeDtypeStruct((devs, 3, held, rows, width), queries.dtype),
        grid=(tubes, steps),
        in_specs=[source, source, source],
        out_specs=pl.BlockSpec((owners, 3, held, step, width), lambda t, i: (t, 0, 0, i, 0)),
        cost_estimate=pl.CostEstimate(
            flops=0, transcendentals=0, bytes_accessed=12 * devs * held * rows * width
        ),
        name="pack",
    )(queries, key_vectors, value_vectors)


def unpack_kernel(src_ref, *refs):
    out_ref = refs[-1]
    step, heads, _ = out_ref.shape
    owners = heads // src_ref.shape[1]
    _, held, _, width = src_ref.shape
    blocks = src_ref[
        pl.ds(pl.program_id(0) * owners, owners), :, pl.ds(pl.program_id(1) * step, step)
    ]
    out_ref[...] = pltpu.einshape("hpd->phd", blocks.reshape(heads, step, width))


def unpack(arrived, out, first, tubes, all_rows):
    devs, held, rows, width = arrived.shape
    owners = devs // tubes
    heads = owners * held
    step = min(rows, 64)
    steps = rows // step
    operands, in_specs, aliases = [arrived], [], {}
    in_specs.append(pl.BlockSpec(memory_space=pltpu.VMEM))
    if out is not None:
        operands.append(out)
        in_specs.append(pl.BlockSpec(memory_space=pl.ANY))
        aliases = {1: 0}
    return pl.pallas_call(
        unpack_kernel,
        out_shape=jax.ShapeDtypeStruct((all_rows, heads, width), arrived.dtype),
        grid=(tubes, steps),
        in_specs=in_specs,
        out_specs=pl.BlockSpec(
            (step, heads, width), lambda t, i: ((first + t) * steps + i, 0, 0)
        ),
        input_output_aliases=aliases,
        cost_estimate=pl.CostEstimate(
            flops=0, transcendentals=0, bytes_accessed=4 * devs * held * rows * width
        ),
        compiler_params=pltpu.CompilerParams(vmem_limit_bytes=24 << 20),
        name="unpack",
    )(*operands)


def attend_kernel(tiles, per_group, plane_tubes, unroll, base_ref, bits_ref, q_ref, k_ref, v_ref, o_ref):
    frames, rows, width = q_ref.shape
    tokens = frames * rows
    span = BLK // rows
    group = 2
    head = base_ref[1] + pl.program_id(0)
    group_tube = head // per_group * plane_tubes + base_ref[0]
    start = group_tube * tiles * per_group + head % per_group
    keys = k_ref[...].reshape(tokens, width)
    values = v_ref[...].reshape(tokens, width)
    block_of = lax.broadcasted_iota(jnp.int32, (1, tokens), 1) // BLK
    scale = width ** (-0.5)

    def step(pair, carry):
        here = pl.ds(pair * group * span, group * span)
        query = q_ref[here].reshape(group * BLK, width)
        scores = lax.dot_general(
            query, keys, (((1,), (1,)), ((), ())), preferred_element_type=jnp.float32
        )
        parts = []
        for member in range(group):
            tile = pair * group + member
            bits = bits_ref[start + tile * per_group]
            chosen = ((bits >> block_of) & 1) == 1
            bias = jnp.where(chosen, 0.0, -jnp.inf)
            part = scores[member * BLK : (member + 1) * BLK] * scale + bias
            weights = jnp.exp(part - jnp.max(part, axis=1, keepdims=True))
            total = jnp.sum(weights, axis=1, keepdims=True)
            parts.append((weights.astype(jnp.bfloat16), total))
        rounded = jnp.concatenate([part for part, _ in parts], axis=0)
        totals = jnp.concatenate([total for _, total in parts], axis=0)
        summed = jnp.dot(rounded, values, preferred_element_type=jnp.float32)
        result = (summed / totals).astype(o_ref.dtype)
        o_ref[here] = result.reshape(group * span, rows, width)
        return carry

    if unroll:
        for pair in range(tiles // group):
            step(pair, 0)
    else:
        lax.fori_loop(0, tiles // group, step, 0)


def attend(arrived, base, bits, tiles, per_group, plane_tubes, unroll):
    devs, _, held, rows, width = arrived.shape
    tokens = devs * rows

    def part(slot):
        return pl.BlockSpec((devs, None, None, rows, width), lambda u, *_: (0, slot, u, 0, 0))

    return pl.pallas_call(
        functools.partial(attend_kernel, tiles, per_group, plane_tubes, unroll),
        out_shape=jax.ShapeDtypeStruct((devs, held, rows, width), arrived.dtype),
        grid_spec=pltpu.PrefetchScalarGridSpec(
            num_scalar_prefetch=2,
            grid=(held,),
            in_specs=[part(2), part(0), part(1)],
            out_specs=pl.BlockSpec((devs, None, rows, width), lambda u, *_: (0, u, 0, 0)),
        ),
        cost_estimate=pl.CostEstimate(
            flops=4 * held * tokens * tokens * width,
            transcendentals=held * tokens * tokens,
            bytes_accessed=8 * held * tokens * width,
        ),
        name="attend",
    )(base, bits, arrived, arrived, arrived)


def attend_own_kernel(q_ref, k_ref, v_ref, o_ref):
    owners, rows, width = q_ref.shape
    scale = width ** (-0.5)
    heads = range(owners)
    scores = [
        lax.dot_general(
            q_ref[h], k_ref[h], (((1,), (1,)), ((), ())), preferred_element_type=jnp.float32
        )
        for h in heads
    ]
    weights, totals = [], []
    for h in heads:
        part = scores[h] * scale
        part = jnp.exp(part - jnp.max(part, axis=1, keepdims=True))
        totals.append(jnp.sum(part, axis=1, keepdims=True))
        weights.append(part.astype(jnp.bfloat16))
    for h in heads:
        summed = jnp.dot(weights[h], v_ref[h], preferred_element_type=jnp.float32)
        o_ref[h] = (summed / totals[h]).astype(o_ref.dtype)


def attend_own(packed):
    owners, _, held, rows, width = packed.shape

    def part(slot):
        return pl.BlockSpec((owners, None, None, rows, width), lambda u: (0, slot, u, 0, 0))

    return pl.pallas_call(
        attend_own_kernel,
        out_shape=jax.ShapeDtypeStruct((owners, held, rows, width), packed.dtype),
        grid=(held,),
        in_specs=[part(2), part(0), part(1)],
        out_specs=pl.BlockSpec((owners, None, rows, width), lambda u: (0, u, 0, 0)),
        cost_estimate=pl.CostEstimate(
            flops=4 * owners * held * rows * rows * width,
            transcendentals=owners * held * rows * rows,
            bytes_accessed=8 * owners * held * rows * width,
        ),
        name="attend_own",
    )(packed, packed, packed)


def gather_kernel(tiles, per_group, plane_tubes, tubes, me_ref, bits_ref, *refs):
    sources, out_ref = refs[:-1], refs[-1]
    owners, _, held, _, _ = sources[0].shape
    me, there = me_ref[0], pl.program_id(0)
    count = jnp.int32(0)
    for tube, source in zip(tubes, sources):

        def step(u, count, tube=tube, source=source):
            for owner in range(owners):
                head = owner * held
                place = (head // per_group * plane_tubes + tube) * tiles * per_group
                bits = bits_ref[place + there * per_group + head % per_group + u]
                chosen = jnp.where(there == me, 0, (bits >> me) & 1)

                @pl.when(chosen == 1)
                def _(count=count, owner=owner):
                    out_ref[count] = source[owner, :, u]

                count = count + chosen
            return count

        count = lax.fori_loop(0, held, step, count)


def gather(me, bits, packed, tubes, cap, tiles, per_group, plane_tubes):
    owners, _, held, rows, width = packed[tubes[0]].shape
    source = pl.BlockSpec((owners, 2, held, rows, width), lambda f, *_: (0, 0, 0, 0, 0))
    return pl.pallas_call(
        functools.partial(gather_kernel, tiles, per_group, plane_tubes, tubes),
        out_shape=jax.ShapeDtypeStruct((owners, cap, 2, rows, width), packed[0].dtype),
        grid_spec=pltpu.PrefetchScalarGridSpec(
            num_scalar_prefetch=2,
            grid=(owners,),
            in_specs=[source] * len(tubes),
            out_specs=pl.BlockSpec((None, cap, 2, rows, width), lambda f, *_: (f, 0, 0, 0, 0)),
        ),
        cost_estimate=pl.CostEstimate(
            flops=0, transcendentals=0, bytes_accessed=8 * owners * cap * rows * width
        ),
        name="gather",
    )(me, bits, *[packed[c] for c in tubes])


def attend_few_kernel(
    tiles, per_group, plane_tubes, tube, me_ref, bits_ref, start_ref, q_ref, k_ref, v_ref, far_ref,
    o_ref, count_ref, slot_ref, keys_ref, values_ref,
):
    owners, rows, width = q_ref.shape
    blocks = far_ref.shape[0]
    held = pl.num_programs(0)
    u, me = pl.program_id(0), me_ref[0]
    scale = width ** (-0.5)

    @pl.when(u == 0)
    def _():
        for b in range(blocks):
            count_ref[b] = start_ref[b]

    def word(owner):
        head = owner * held
        place = (head // per_group * plane_tubes + tube) * tiles * per_group
        return bits_ref[place + me * per_group + head % per_group + u]

    counts = [count_ref[b] for b in range(blocks)]
    most, pick = jnp.int32(0), []
    for owner in range(owners):
        bits = word(owner)
        number, at, slot = jnp.int32(0), jnp.int32(0), jnp.int32(0)
        for b in range(blocks):
            chosen = jnp.where(me == b, 0, (bits >> b) & 1)
            slot_ref[owner * blocks + b] = counts[b]
            at = jnp.where(chosen == 1, b, at)
            slot = jnp.where(chosen == 1, counts[b], slot)
            counts[b] = counts[b] + chosen
            number = number + chosen
        most = jnp.maximum(most, number)
        pick.append((number, at, slot))
        bits_of = bits
        slot_ref[owners * blocks + owner] = bits_of
    for b in range(blocks):
        count_ref[b] = counts[b]

    def normal(scores):
        weights = jnp.exp(scores - jnp.max(scores, axis=1, keepdims=True))
        total = jnp.sum(weights, axis=1, keepdims=True)
        return weights.astype(jnp.bfloat16), total

    @pl.when(most <= 1)
    def _():
        lane = lax.broadcasted_iota(jnp.int32, (1, 2 * rows), 1)
        scores, values = [], []
        for owner, (number, at, slot) in enumerate(pick):
            far = number == 1
            key, value = k_ref[owner], v_ref[owner]
            keys = jnp.concatenate([key, jnp.where(far, far_ref[at, slot, 0], key)], axis=0)
            values.append(
                jnp.concatenate([value, jnp.where(far, far_ref[at, slot, 1], value)], axis=0)
            )
            part = lax.dot_general(
                q_ref[owner], keys, (((1,), (1,)), ((), ())), preferred_element_type=jnp.float32
            )
            bias = jnp.where(lane < rows + rows * number, 0.0, -jnp.inf)
            scores.append(part * scale + bias)
        parts = [normal(part) for part in scores]
        for owner, (weights, total) in enumerate(parts):
            summed = jnp.dot(weights, values[owner], preferred_element_type=jnp.float32)
            o_ref[owner] = (summed / total).astype(o_ref.dtype)

    @pl.when(most > 1)
    def _():
        block_of = lax.broadcasted_iota(jnp.int32, (1, blocks * rows), 1) // rows

        def one(owner, carry):
            bits = slot_ref[owners * blocks + owner]
            for b in range(blocks):
                far = jnp.where(me == b, 0, (bits >> b) & 1) == 1
                here = slice(b * rows, (b + 1) * rows)

                @pl.when(far)
                def _(b=b, here=here):
                    slot = slot_ref[owner * blocks + b]
                    keys_ref[here] = far_ref[b, slot, 0]
                    values_ref[here] = far_ref[b, slot, 1]

                @pl.when(jnp.logical_not(far))
                def _(here=here):
                    keys_ref[here] = k_ref[owner]
                    values_ref[here] = v_ref[owner]

            bias = jnp.where(((bits >> block_of) & 1) == 1, 0.0, -jnp.inf)
            part = lax.dot_general(
                q_ref[owner],
                keys_ref[...],
                (((1,), (1,)), ((), ())),
                preferred_element_type=jnp.float32,
            )
            weights, total = normal(part * scale + bias)
            summed = jnp.dot(weights, values_ref[...], preferred_element_type=jnp.float32)
            o_ref[owner] = (summed / total).astype(o_ref.dtype)
            return carry

        lax.fori_loop(0, owners, one, 0)


def attend_few(me, bits, start, packed, far, tube, tiles, per_group, plane_tubes):
    owners, _, held, rows, width = packed.shape
    blocks, cap = far.shape[:2]

    def part(slot):
        return pl.BlockSpec((owners, None, None, rows, width), lambda u, *_: (0, slot, u, 0, 0))

    return pl.pallas_call(
        functools.partial(attend_few_kernel, tiles, per_group, plane_tubes, tube),
        out_shape=jax.ShapeDtypeStruct((owners, held, rows, width), packed.dtype),
        grid_spec=pltpu.PrefetchScalarGridSpec(
            num_scalar_prefetch=3,
            grid=(held,),
            in_specs=[
                part(2),
                part(0),
                part(1),
                pl.BlockSpec(far.shape, lambda u, *_: (0, 0, 0, 0, 0)),
            ],
            out_specs=pl.BlockSpec((owners, None, rows, width), lambda u, *_: (0, u, 0, 0)),
            scratch_shapes=[
                pltpu.SMEM((blocks,), jnp.int32),
                pltpu.SMEM((owners * (blocks + 1),), jnp.int32),
                pltpu.VMEM((blocks * rows, width), packed.dtype),
                pltpu.VMEM((blocks * rows, width), packed.dtype),
            ],
        ),
        cost_estimate=pl.CostEstimate(
            flops=8 * owners * held * rows * rows * width,
            transcendentals=2 * owners * held * rows * rows,
            bytes_accessed=8 * owners * held * rows * width + 4 * blocks * cap * rows * width,
        ),
        name="attend_few",
    )(me, bits, start, packed, packed, packed, far)


def exchange(blocks):
    return lax.all_to_all(blocks, "st", split_axis=0, concat_axis=0, tiled=True)


def body(queries, key_vectors, value_vectors, block_lists):
    head_devs = lax.axis_size("head")
    st_devs = lax.axis_size("st")
    local_frames, local_space, heads, width = queries.shape
    plane_tubes = st_devs // head_devs
    rows = local_frames * local_space // plane_tubes
    tiles, per_group, entries = block_lists.shape
    all_rows = local_frames * local_space
    chunk_tubes = 1 if heads % st_devs == 0 else plane_tubes
    held = chunk_tubes * heads // st_devs
    owners = st_devs // chunk_tubes
    chunks = plane_tubes // chunk_tubes

    def flat(source):
        shaped = source.reshape(local_frames, plane_tubes, -1, heads, width)
        return jnp.swapaxes(shaped, 0, 1).reshape(all_rows, heads, width)

    tensors = flat(queries), flat(key_vectors), flat(value_vectors)
    head_at, st_at = lax.axis_index("head"), lax.axis_index("st")
    tile_size = tiles * per_group
    mine = jnp.broadcast_to(block_lists.reshape(1, 1, -1), (head_devs * st_devs, 1, block_lists.size))
    every = lax.all_to_all(mine, ("head", "st"), split_axis=0, concat_axis=0, tiled=True)
    every = every.reshape(head_devs, st_devs, block_lists.size)
    lists = lax.dynamic_slice_in_dim(every, head_at * plane_tubes, plane_tubes, 1)
    values = jnp.where(lists >= 0, 1 << jnp.maximum(lists, 0), 0).astype(jnp.float32)
    words = tile_size
    joins = jnp.arange(words * entries)[:, None] // entries == jnp.arange(words)[None]
    bits = jnp.dot(
        values.reshape(-1, words * entries),
        joins.astype(jnp.float32),
        precision=lax.Precision.HIGHEST,
    )
    bits = bits.astype(jnp.int32).reshape(-1)
    packed = [
        pack(*tensors, c * chunk_tubes, chunk_tubes, rows, st_devs) for c in range(chunks)
    ]
    me = jnp.stack([st_at])

    def run(whole, few, cap, packed, bits, counts):
        out, arrived, far = None, {}, None
        for c in whole:
            arrived[c] = exchange(packed[c])
        if few:
            far = exchange(gather(me, bits, packed, few, cap, tiles, per_group, plane_tubes))
        for c in range(chunks):
            if c not in whole and c not in few:
                result = attend_own(packed[c])
                out = unpack(result, out, c * chunk_tubes, chunk_tubes, all_rows)
        for c in whole:
            blocks = arrived[c]
            if out is not None and len(whole) < chunks:
                blocks, out = lax.optimization_barrier((blocks, out))
            base = jnp.stack([c + st_at // owners, (st_at % owners) * held])
            alone = len(whole) == 1 and not few
            result = attend(blocks, base, bits, tiles, per_group, plane_tubes, alone)
            arrived[c] = exchange(result)
        start = jnp.zeros_like(counts[0])
        for c in few:
            result = attend_few(me, bits, start, packed[c], far, c, tiles, per_group, plane_tubes)
            start = start + counts[c]
            out = unpack(result, out, c * chunk_tubes, chunk_tubes, all_rows)
        for c in whole:
            out = unpack(arrived[c], out, c * chunk_tubes, chunk_tubes, all_rows)
        return out

    few_possible = rows == BLK and tiles == st_devs and chunk_tubes == 1
    if few_possible and plane_tubes == 2 and per_group % held == 0:
        tile_of = jnp.arange(words * entries) // (per_group * entries)
        hits = lists[:, :, None] == jnp.arange(tiles)[None, None, :, None]
        spread = tile_of[:, None] == jnp.arange(tiles)
        need = jnp.einsum(
            "gcbl,lt->cbt",
            hits.astype(jnp.bfloat16),
            spread.astype(jnp.bfloat16),
            preferred_element_type=jnp.float32,
        )
        need = jnp.where(jnp.eye(tiles, dtype=bool)[None], 0.0, need)
        counts = jnp.sum(jnp.where(jnp.arange(tiles) == st_at, need, 0.0), axis=2)
        counts = counts.astype(jnp.int32)
        one_cap, two_cap = heads // 5, heads // 3
        most = jnp.max(jnp.concatenate([need, need[:1] + need[1:]]), axis=(1, 2))
        bound = jnp.where(jnp.arange(3) == 2, two_cap, one_cap)
        level = jnp.where(most == 0, 0, jnp.where(most <= bound, 1, 2))
        code = jnp.sum(level << (2 * jnp.arange(3)))
        a, b, both = code & 3, (code >> 2) & 3, code >> 4
        pair = (a > 0) & (b > 0) & (both <= 1)
        a = jnp.where((a == 1) & (b == 1), 2, a)
        which = jnp.where(pair, 4, a * 3 + b)
        plans = [
            ((), (), 0),
            ((), (1,), one_cap),
            ((1,), (), 0),
            ((), (0,), one_cap),
            ((), (0, 1), two_cap),
            ((1,), (0,), one_cap),
            ((0,), (), 0),
            ((0,), (1,), one_cap),
            ((0, 1), (), 0),
        ]

        def branch(plan):
            return lambda packed, bits, counts: run(*plan, packed, bits, counts)

        out = lax.switch(which, [branch(plan) for plan in plans], packed, bits, counts)
    else:
        none = [jnp.zeros((tiles,), jnp.int32)]
        out = run(tuple(range(chunks)), (), 0, packed, bits, none)
    shaped = out.reshape(plane_tubes, local_frames, -1, heads, width)
    return jnp.swapaxes(shaped, 0, 1).reshape(queries.shape)


def solution(mesh):
    spec = P("st", "head", None, None)
    return jax.shard_map(
        body,
        mesh=mesh,
        in_specs=(spec, spec, spec, P("st", "head", None)),
        out_specs=spec,
        check_vma=False,
    )
```

```python
import functools

import jax
import jax.numpy as jnp
from jax import lax
from jax.experimental import pallas as pl
from jax.experimental.pallas import tpu as pltpu
from jax.sharding import PartitionSpec as P

BLK = 128


def pack_kernel(q_ref, k_ref, v_ref, out_ref):
    owners, _, held, rows, width = out_ref.shape
    for slot, ref in enumerate((k_ref, v_ref, q_ref)):
        turned = pltpu.einshape("phd->hpd", ref[...])
        out_ref[:, slot] = turned.reshape(owners, held, rows, width)


def pack(queries, key_vectors, value_vectors, first, tubes, rows, devs):
    heads, width = queries.shape[1:]
    held = tubes * heads // devs
    owners = heads // held
    step = min(rows, 64)
    steps = rows // step
    source = pl.BlockSpec((step, heads, width), lambda t, i: ((first + t) * steps + i, 0, 0))
    return pl.pallas_call(
        pack_kernel,
        out_shape=jax.ShapeDtypeStruct((devs, 3, held, rows, width), queries.dtype),
        grid=(tubes, steps),
        in_specs=[source, source, source],
        out_specs=pl.BlockSpec((owners, 3, held, step, width), lambda t, i: (t, 0, 0, i, 0)),
        cost_estimate=pl.CostEstimate(
            flops=0, transcendentals=0, bytes_accessed=12 * devs * held * rows * width
        ),
        name="pack",
    )(queries, key_vectors, value_vectors)


def unpack_kernel(src_ref, *refs):
    out_ref = refs[-1]
    step, heads, _ = out_ref.shape
    owners = heads // src_ref.shape[1]
    _, held, _, width = src_ref.shape
    blocks = src_ref[
        pl.ds(pl.program_id(0) * owners, owners), :, pl.ds(pl.program_id(1) * step, step)
    ]
    out_ref[...] = pltpu.einshape("hpd->phd", blocks.reshape(heads, step, width))


def unpack(arrived, out, first, tubes, all_rows):
    devs, held, rows, width = arrived.shape
    owners = devs // tubes
    heads = owners * held
    step = min(rows, 64)
    steps = rows // step
    operands, in_specs, aliases = [arrived], [], {}
    in_specs.append(pl.BlockSpec(memory_space=pltpu.VMEM))
    if out is not None:
        operands.append(out)
        in_specs.append(pl.BlockSpec(memory_space=pl.ANY))
        aliases = {1: 0}
    return pl.pallas_call(
        unpack_kernel,
        out_shape=jax.ShapeDtypeStruct((all_rows, heads, width), arrived.dtype),
        grid=(tubes, steps),
        in_specs=in_specs,
        out_specs=pl.BlockSpec(
            (step, heads, width), lambda t, i: ((first + t) * steps + i, 0, 0)
        ),
        input_output_aliases=aliases,
        cost_estimate=pl.CostEstimate(
            flops=0, transcendentals=0, bytes_accessed=4 * devs * held * rows * width
        ),
        compiler_params=pltpu.CompilerParams(vmem_limit_bytes=24 << 20),
        name="unpack",
    )(*operands)


def attend_kernel(tiles, per_group, plane_tubes, unroll, base_ref, bits_ref, q_ref, k_ref, v_ref, o_ref):
    frames, rows, width = q_ref.shape
    tokens = frames * rows
    span = BLK // rows
    group = 2
    head = base_ref[1] + pl.program_id(0)
    group_tube = head // per_group * plane_tubes + base_ref[0]
    start = group_tube * tiles * per_group + head % per_group
    keys = k_ref[...].reshape(tokens, width)
    values = v_ref[...].reshape(tokens, width)
    block_of = lax.broadcasted_iota(jnp.int32, (1, tokens), 1) // BLK
    scale = width ** (-0.5)

    def step(pair, carry):
        here = pl.ds(pair * group * span, group * span)
        query = q_ref[here].reshape(group * BLK, width)
        scores = lax.dot_general(
            query, keys, (((1,), (1,)), ((), ())), preferred_element_type=jnp.float32
        )
        parts = []
        for member in range(group):
            tile = pair * group + member
            bits = bits_ref[start + tile * per_group]
            chosen = ((bits >> block_of) & 1) == 1
            bias = jnp.where(chosen, 0.0, -jnp.inf)
            part = scores[member * BLK : (member + 1) * BLK] * scale + bias
            weights = jnp.exp(part - jnp.max(part, axis=1, keepdims=True))
            total = jnp.sum(weights, axis=1, keepdims=True)
            parts.append((weights.astype(jnp.bfloat16), total))
        rounded = jnp.concatenate([part for part, _ in parts], axis=0)
        totals = jnp.concatenate([total for _, total in parts], axis=0)
        summed = jnp.dot(rounded, values, preferred_element_type=jnp.float32)
        result = (summed / totals).astype(o_ref.dtype)
        o_ref[here] = result.reshape(group * span, rows, width)
        return carry

    if unroll:
        for pair in range(tiles // group):
            step(pair, 0)
    else:
        lax.fori_loop(0, tiles // group, step, 0)


def attend(arrived, base, bits, tiles, per_group, plane_tubes, unroll):
    devs, _, held, rows, width = arrived.shape
    tokens = devs * rows

    def part(slot):
        return pl.BlockSpec((devs, None, None, rows, width), lambda u, *_: (0, slot, u, 0, 0))

    return pl.pallas_call(
        functools.partial(attend_kernel, tiles, per_group, plane_tubes, unroll),
        out_shape=jax.ShapeDtypeStruct((devs, held, rows, width), arrived.dtype),
        grid_spec=pltpu.PrefetchScalarGridSpec(
            num_scalar_prefetch=2,
            grid=(held,),
            in_specs=[part(2), part(0), part(1)],
            out_specs=pl.BlockSpec((devs, None, rows, width), lambda u, *_: (0, u, 0, 0)),
        ),
        cost_estimate=pl.CostEstimate(
            flops=4 * held * tokens * tokens * width,
            transcendentals=held * tokens * tokens,
            bytes_accessed=8 * held * tokens * width,
        ),
        name="attend",
    )(base, bits, arrived, arrived, arrived)


def attend_own_kernel(q_ref, k_ref, v_ref, o_ref):
    owners, rows, width = q_ref.shape
    scale = width ** (-0.5)
    heads = range(owners)
    scores = [
        lax.dot_general(
            q_ref[h], k_ref[h], (((1,), (1,)), ((), ())), preferred_element_type=jnp.float32
        )
        for h in heads
    ]
    weights, totals = [], []
    for h in heads:
        part = scores[h] * scale
        part = jnp.exp(part - jnp.max(part, axis=1, keepdims=True))
        totals.append(jnp.sum(part, axis=1, keepdims=True))
        weights.append(part.astype(jnp.bfloat16))
    for h in heads:
        summed = jnp.dot(weights[h], v_ref[h], preferred_element_type=jnp.float32)
        o_ref[h] = (summed / totals[h]).astype(o_ref.dtype)


def attend_own(packed):
    owners, _, held, rows, width = packed.shape

    def part(slot):
        return pl.BlockSpec((owners, None, None, rows, width), lambda u: (0, slot, u, 0, 0))

    return pl.pallas_call(
        attend_own_kernel,
        out_shape=jax.ShapeDtypeStruct((owners, held, rows, width), packed.dtype),
        grid=(held,),
        in_specs=[part(2), part(0), part(1)],
        out_specs=pl.BlockSpec((owners, None, rows, width), lambda u: (0, u, 0, 0)),
        cost_estimate=pl.CostEstimate(
            flops=4 * owners * held * rows * rows * width,
            transcendentals=owners * held * rows * rows,
            bytes_accessed=8 * owners * held * rows * width,
        ),
        compiler_params=pltpu.CompilerParams(vmem_limit_bytes=24 << 20),
        name="attend_own",
    )(packed, packed, packed)


def gather_kernel(tiles, per_group, plane_tubes, tubes, me_ref, bits_ref, *refs):
    sources, out_ref = refs[:-1], refs[-1]
    owners, _, held, _, _ = sources[0].shape
    me, there = me_ref[0], pl.program_id(0)
    count = jnp.int32(0)
    for tube, source in zip(tubes, sources):

        def step(u, count, tube=tube, source=source):
            for owner in range(owners):
                head = owner * held
                place = (head // per_group * plane_tubes + tube) * tiles * per_group
                bits = bits_ref[place + there * per_group + head % per_group + u]
                chosen = jnp.where(there == me, 0, (bits >> me) & 1)

                @pl.when(chosen == 1)
                def _(count=count, owner=owner):
                    out_ref[count] = source[owner, :, u]

                count = count + chosen
            return count

        count = lax.fori_loop(0, held, step, count)


def gather(me, bits, packed, tubes, cap, tiles, per_group, plane_tubes):
    owners, _, held, rows, width = packed[tubes[0]].shape
    source = pl.BlockSpec((owners, 2, held, rows, width), lambda f, *_: (0, 0, 0, 0, 0))
    return pl.pallas_call(
        functools.partial(gather_kernel, tiles, per_group, plane_tubes, tubes),
        out_shape=jax.ShapeDtypeStruct((owners, cap, 2, rows, width), packed[0].dtype),
        grid_spec=pltpu.PrefetchScalarGridSpec(
            num_scalar_prefetch=2,
            grid=(owners,),
            in_specs=[source] * len(tubes),
            out_specs=pl.BlockSpec((None, cap, 2, rows, width), lambda f, *_: (f, 0, 0, 0, 0)),
        ),
        cost_estimate=pl.CostEstimate(
            flops=0, transcendentals=0, bytes_accessed=8 * owners * cap * rows * width
        ),
        compiler_params=pltpu.CompilerParams(vmem_limit_bytes=24 << 20),
        name="gather",
    )(me, bits, *[packed[c] for c in tubes])


def attend_few_kernel(
    tiles, per_group, plane_tubes, tube, me_ref, bits_ref, start_ref, q_ref, k_ref, v_ref, far_ref,
    o_ref, count_ref, slot_ref, keys_ref, values_ref,
):
    owners, rows, width = q_ref.shape
    blocks = far_ref.shape[0]
    held = pl.num_programs(0)
    u, me = pl.program_id(0), me_ref[0]
    scale = width ** (-0.5)

    @pl.when(u == 0)
    def _():
        for b in range(blocks):
            count_ref[b] = start_ref[b]

    def word(owner):
        head = owner * held
        place = (head // per_group * plane_tubes + tube) * tiles * per_group
        return bits_ref[place + me * per_group + head % per_group + u]

    counts = [count_ref[b] for b in range(blocks)]
    most, pick = jnp.int32(0), []
    for owner in range(owners):
        bits = word(owner)
        number, at, slot = jnp.int32(0), jnp.int32(0), jnp.int32(0)
        for b in range(blocks):
            chosen = jnp.where(me == b, 0, (bits >> b) & 1)
            slot_ref[owner * blocks + b] = counts[b]
            at = jnp.where(chosen == 1, b, at)
            slot = jnp.where(chosen == 1, counts[b], slot)
            counts[b] = counts[b] + chosen
            number = number + chosen
        most = jnp.maximum(most, number)
        pick.append((number, at, slot))
        bits_of = bits
        slot_ref[owners * blocks + owner] = bits_of
    for b in range(blocks):
        count_ref[b] = counts[b]

    def normal(scores):
        weights = jnp.exp(scores - jnp.max(scores, axis=1, keepdims=True))
        total = jnp.sum(weights, axis=1, keepdims=True)
        return weights.astype(jnp.bfloat16), total

    @pl.when(most <= 1)
    def _():
        lane = lax.broadcasted_iota(jnp.int32, (1, 2 * rows), 1)
        scores, values = [], []
        for owner, (number, at, slot) in enumerate(pick):
            far = number == 1
            key, value = k_ref[owner], v_ref[owner]
            keys = jnp.concatenate([key, jnp.where(far, far_ref[at, slot, 0], key)], axis=0)
            values.append(
                jnp.concatenate([value, jnp.where(far, far_ref[at, slot, 1], value)], axis=0)
            )
            part = lax.dot_general(
                q_ref[owner], keys, (((1,), (1,)), ((), ())), preferred_element_type=jnp.float32
            )
            bias = jnp.where(lane < rows + rows * number, 0.0, -jnp.inf)
            scores.append(part * scale + bias)
        parts = [normal(part) for part in scores]
        for owner, (weights, total) in enumerate(parts):
            summed = jnp.dot(weights, values[owner], preferred_element_type=jnp.float32)
            o_ref[owner] = (summed / total).astype(o_ref.dtype)

    @pl.when(most > 1)
    def _():
        block_of = lax.broadcasted_iota(jnp.int32, (1, blocks * rows), 1) // rows

        def one(owner, carry):
            bits = slot_ref[owners * blocks + owner]

            def fill(b, carry):
                far = jnp.where(me == b, 0, (bits >> b) & 1) == 1
                here = pl.ds(pl.multiple_of(b * rows, rows), rows)

                @pl.when(far)
                def _():
                    slot = slot_ref[owner * blocks + b]
                    keys_ref[here] = far_ref[b, slot, 0]
                    values_ref[here] = far_ref[b, slot, 1]

                @pl.when(jnp.logical_not(far))
                def _():
                    keys_ref[here] = k_ref[owner]
                    values_ref[here] = v_ref[owner]

                return carry

            lax.fori_loop(0, blocks, fill, 0)
            bias = jnp.where(((bits >> block_of) & 1) == 1, 0.0, -jnp.inf)
            part = lax.dot_general(
                q_ref[owner],
                keys_ref[...],
                (((1,), (1,)), ((), ())),
                preferred_element_type=jnp.float32,
            )
            weights, total = normal(part * scale + bias)
            summed = jnp.dot(weights, values_ref[...], preferred_element_type=jnp.float32)
            o_ref[owner] = (summed / total).astype(o_ref.dtype)
            return carry

        lax.fori_loop(0, owners, one, 0)


def attend_few(me, bits, start, packed, far, tube, tiles, per_group, plane_tubes):
    owners, _, held, rows, width = packed.shape
    blocks, cap = far.shape[:2]

    def part(slot):
        return pl.BlockSpec((owners, None, None, rows, width), lambda u, *_: (0, slot, u, 0, 0))

    return pl.pallas_call(
        functools.partial(attend_few_kernel, tiles, per_group, plane_tubes, tube),
        out_shape=jax.ShapeDtypeStruct((owners, held, rows, width), packed.dtype),
        grid_spec=pltpu.PrefetchScalarGridSpec(
            num_scalar_prefetch=3,
            grid=(held,),
            in_specs=[
                part(2),
                part(0),
                part(1),
                pl.BlockSpec(far.shape, lambda u, *_: (0, 0, 0, 0, 0)),
            ],
            out_specs=pl.BlockSpec((owners, None, rows, width), lambda u, *_: (0, u, 0, 0)),
            scratch_shapes=[
                pltpu.SMEM((blocks,), jnp.int32),
                pltpu.SMEM((owners * (blocks + 1),), jnp.int32),
                pltpu.VMEM((blocks * rows, width), packed.dtype),
                pltpu.VMEM((blocks * rows, width), packed.dtype),
            ],
        ),
        cost_estimate=pl.CostEstimate(
            flops=8 * owners * held * rows * rows * width,
            transcendentals=2 * owners * held * rows * rows,
            bytes_accessed=8 * owners * held * rows * width + 4 * blocks * cap * rows * width,
        ),
        compiler_params=pltpu.CompilerParams(vmem_limit_bytes=24 << 20),
        name="attend_few",
    )(me, bits, start, packed, packed, packed, far)


def exchange(blocks):
    return lax.all_to_all(blocks, "st", split_axis=0, concat_axis=0, tiled=True)


def body(queries, key_vectors, value_vectors, block_lists):
    head_devs = lax.axis_size("head")
    st_devs = lax.axis_size("st")
    local_frames, local_space, heads, width = queries.shape
    plane_tubes = st_devs // head_devs
    rows = local_frames * local_space // plane_tubes
    tiles, per_group, entries = block_lists.shape
    all_rows = local_frames * local_space
    chunk_tubes = 1 if heads % st_devs == 0 else plane_tubes
    held = chunk_tubes * heads // st_devs
    owners = st_devs // chunk_tubes
    chunks = plane_tubes // chunk_tubes

    def flat(source):
        shaped = source.reshape(local_frames, plane_tubes, -1, heads, width)
        return jnp.swapaxes(shaped, 0, 1).reshape(all_rows, heads, width)

    tensors = flat(queries), flat(key_vectors), flat(value_vectors)
    head_at, st_at = lax.axis_index("head"), lax.axis_index("st")
    tile_size = tiles * per_group
    mine = jnp.broadcast_to(block_lists.reshape(1, 1, -1), (head_devs * st_devs, 1, block_lists.size))
    every = lax.all_to_all(mine, ("head", "st"), split_axis=0, concat_axis=0, tiled=True)
    every = every.reshape(head_devs, st_devs, block_lists.size)
    lists = lax.dynamic_slice_in_dim(every, head_at * plane_tubes, plane_tubes, 1)
    values = jnp.where(lists >= 0, 1 << jnp.maximum(lists, 0), 0).astype(jnp.float32)
    words = tile_size
    joins = jnp.arange(words * entries)[:, None] // entries == jnp.arange(words)[None]
    bits = jnp.dot(
        values.reshape(-1, words * entries),
        joins.astype(jnp.float32),
        precision=lax.Precision.HIGHEST,
    )
    bits = bits.astype(jnp.int32).reshape(-1)
    packed = [
        pack(*tensors, c * chunk_tubes, chunk_tubes, rows, st_devs) for c in range(chunks)
    ]
    me = jnp.stack([st_at])

    def run(whole, few, cap, packed, bits, counts):
        out, arrived, far = None, {}, None
        for c in whole:
            arrived[c] = exchange(packed[c])
        if few:
            far = exchange(gather(me, bits, packed, few, cap, tiles, per_group, plane_tubes))
        for c in range(chunks):
            if c not in whole and c not in few:
                result = attend_own(packed[c])
                out = unpack(result, out, c * chunk_tubes, chunk_tubes, all_rows)
        for c in whole:
            blocks = arrived[c]
            if out is not None and len(whole) < chunks:
                blocks, out = lax.optimization_barrier((blocks, out))
            base = jnp.stack([c + st_at // owners, (st_at % owners) * held])
            result = attend(blocks, base, bits, tiles, per_group, plane_tubes, not few)
            arrived[c] = exchange(result)
        start = jnp.zeros_like(counts[0])
        for c in few:
            result = attend_few(me, bits, start, packed[c], far, c, tiles, per_group, plane_tubes)
            start = start + counts[c]
            out = unpack(result, out, c * chunk_tubes, chunk_tubes, all_rows)
        for c in whole:
            out = unpack(arrived[c], out, c * chunk_tubes, chunk_tubes, all_rows)
        return out

    few_possible = rows == BLK and tiles == st_devs and chunk_tubes == 1
    if few_possible and plane_tubes == 2 and per_group % held == 0:
        tile_of = jnp.arange(words * entries) // (per_group * entries)
        hits = lists[:, :, None] == jnp.arange(tiles)[None, None, :, None]
        spread = tile_of[:, None] == jnp.arange(tiles)
        need = jnp.einsum(
            "gcbl,lt->cbt",
            hits.astype(jnp.bfloat16),
            spread.astype(jnp.bfloat16),
            preferred_element_type=jnp.float32,
        )
        need = jnp.where(jnp.eye(tiles, dtype=bool)[None], 0.0, need)
        counts = jnp.sum(jnp.where(jnp.arange(tiles) == st_at, need, 0.0), axis=2)
        counts = counts.astype(jnp.int32)
        one_cap, two_cap = heads // 5, heads // 3
        most = jnp.max(jnp.concatenate([need, need[:1] + need[1:]]), axis=(1, 2))
        bound = jnp.where(jnp.arange(3) == 2, two_cap, one_cap)
        level = jnp.where(most == 0, 0, jnp.where(most <= bound, 1, 2))
        code = jnp.sum(level << (2 * jnp.arange(3)))
        a, b, both = code & 3, (code >> 2) & 3, code >> 4
        pair = (a > 0) & (b > 0) & (both <= 1)
        a = jnp.where((a == 1) & (b == 1), 2, a)
        which = jnp.where(pair, 4, a * 3 + b)
        plans = [
            ((), (), 0),
            ((), (1,), one_cap),
            ((1,), (), 0),
            ((), (0,), one_cap),
            ((), (0, 1), two_cap),
            ((1,), (0,), one_cap),
            ((0,), (), 0),
            ((0,), (1,), one_cap),
            ((0, 1), (), 0),
        ]

        def branch(plan):
            return lambda packed, bits, counts: run(*plan, packed, bits, counts)

        out = lax.switch(which, [branch(plan) for plan in plans], packed, bits, counts)
    else:
        none = [jnp.zeros((tiles,), jnp.int32)]
        out = run(tuple(range(chunks)), (), 0, packed, bits, none)
    shaped = out.reshape(plane_tubes, local_frames, -1, heads, width)
    return jnp.swapaxes(shaped, 0, 1).reshape(queries.shape)


def solution(mesh):
    spec = P("st", "head", None, None)
    return jax.shard_map(
        body,
        mesh=mesh,
        in_specs=(spec, spec, spec, P("st", "head", None)),
        out_specs=spec,
        check_vma=False,
    )
```
